32 devices in a mesh: member: 8 (over y, x, core), tile: 4 (over z).
Axes of the slice: x: 2, y: 2, z: 4, core: 2. Of those that a mesh axis runs over, the one named last changes fastest.
Arguments:
- node_fine: int32 [8, 12], P('member'), may hold values from 0 to 8
- node_coarse: int32 [32, 12], P('member'), may hold values from 0 to 8
- weight_fine: int32 [8], P('member'), may hold values from -3 to 3
- weight_coarse: int32 [32], P('member'), may hold values from -3 to 3
- mode_x: float32 [12, 64], replicated, may hold values from -1 to 1
- mode_y: float32 [12, 512], replicated, may hold values from -1 to 1
- mode_z: float32 [12, 32], replicated, may hold values from -1 to 1
- source_fine: float32 [64, 32, 512], P('tile'), may hold values from -12 to 12
- source_coarse: float32 [32, 16, 256], P(None, None, 'tile'), may hold values from -6 to 6
Outputs:
- combined: float32 [32, 16, 256], P('member', None, 'tile')
The draws below stay inside these ranges and needn't reach their ends.
All inputs are finite; a program needn't handle non-finite values.
Results may differ from the reference program's by a relative error of at most 0.00026.
Values sent between devices are 32-bit elements; how exact they have to be, the bound alone decides.
No kernel may reach another device: no remote copies, remote signals or barrier semaphores. Data moves between devices by JAX's collectives and lax.ppermute only.
A program may use at most 192 MiB of HBM per device.

```python
import math
import jax
import jax.numpy as jnp
from jax import lax

KL = 12
NODES = 9
SWEEPS = 3
NZF = 32
NYF = 512
FINE = 8
COARSE = 32
NXF = 64
NXC = 32
NZC = 16
NYC = 256


def with_ends(array, stream_key, low, top_value):
    shape = array.shape
    place = [jax.random.randint(jax.random.fold_in(stream_key, axis), (), 0, shape[axis]) for axis in range(len(shape))]
    array = array.at[tuple(place)].set(low)
    longest = shape.index(max(shape))
    place[longest] = (place[longest] + 1) % shape[longest]
    return array.at[tuple(place)].set(top_value)


def levels(stream_key, dims, cuts, smallest, largest):
    loudness = 1.0
    for position, parts in cuts:
        heights = jax.random.uniform(jax.random.fold_in(jax.random.fold_in(stream_key, 6), position), (parts,), jnp.float32, smallest / len(cuts), largest / len(cuts))
        loudness = loudness * jnp.repeat(jnp.exp(heights), dims[position] // parts).reshape((-1,) + (1,) * (len(dims) - 1 - position))
    return loudness


def scatter_about(own_key, shape, scale, limit, shards=(), dtype=jnp.bfloat16):
    values = jax.random.normal(own_key, shape, jnp.float32) * scale
    if len(shards) > 0:
        values = levels(own_key, shape, shards, -0.22, 0.18) * values
    return jnp.clip(values, min=-limit, max=limit).astype(dtype)


def setup_inputs(seed: int = 0) -> dict:
    key_of = jax.random.split(jax.random.key(seed), 10)
    node_fine = with_ends(jax.random.randint(key_of[0], (FINE, KL), 0, NODES), jax.random.fold_in(key_of[0], 1), 0, NODES - 1).astype(jnp.int32)
    node_coarse = with_ends(jax.random.randint(key_of[1], (COARSE, KL), 0, NODES), jax.random.fold_in(key_of[1], 1), 0, NODES - 1).astype(jnp.int32)
    weight_fine = with_ends(jax.random.randint(key_of[2], (FINE,), -3, 4), jax.random.fold_in(key_of[2], 1), -3, 3).astype(jnp.int32)
    weight_coarse = with_ends(jax.random.randint(key_of[3], (COARSE,), -3, 4), jax.random.fold_in(key_of[3], 1), -3, 3).astype(jnp.int32)
    mode_x = jnp.clip(jax.random.uniform(key_of[4], (KL, NXF), jnp.float32, -1.0, 1.0), -1.0, 1.0)
    mode_y = jnp.clip(jax.random.uniform(key_of[5], (KL, NYF), jnp.float32, -1.0, 1.0), -1.0, 1.0)
    mode_z = jnp.clip(jax.random.uniform(key_of[6], (KL, NZF), jnp.float32, -1.0, 1.0), -1.0, 1.0)
    source_fine = scatter_about(key_of[7], (NXF, NZF, NYF), 2.0, 12.0, ((0, 4),), jnp.float32)
    source_coarse = scatter_about(key_of[8], (NXC, NZC, NYC), 1.0, 6.0, ((2, 4),), jnp.float32)
    return dict(node_fine=node_fine, node_coarse=node_coarse, weight_fine=weight_fine, weight_coarse=weight_coarse, mode_x=mode_x, mode_y=mode_y, mode_z=mode_z, source_fine=source_fine, source_coarse=source_coarse)


CENTRE = 1.125
HALF_WIDTH = 0.875
SPREAD_RATIO = CENTRE / HALF_WIDTH


def sweep_factors(sweep_count):
    previous = 1.0 / SPREAD_RATIO
    factors = []
    for _ in range(sweep_count - 1):
        current = 1.0 / (2.0 * SPREAD_RATIO - previous)
        factors.append((current * previous, 2.0 * current / HALF_WIDTH))
        previous = current
    return factors


def shifted(tensor, spatial, along_dim, offset):
    for current in spatial:
        begin_at = offset if current == along_dim else 1
        tensor = lax.slice_in_dim(tensor, begin_at, tensor.shape[current] - 2 + begin_at, axis=current)
    return tensor


def diagonal_of(cond_pad, spatial):
    centre = shifted(cond_pad, spatial, -1, 1)
    running = jnp.zeros_like(centre)
    for along_dim in spatial:
        for offset in (0, 2):
            running = running + 0.5 * (centre + shifted(cond_pad, spatial, along_dim, offset))
    return running


def apply_op(field_pad, cond_pad, spatial):
    centre_k = shifted(cond_pad, spatial, -1, 1)
    centre_v = shifted(field_pad, spatial, -1, 1)
    running = jnp.zeros_like(centre_v * centre_k)
    for along_dim in spatial:
        for offset in (0, 2):
            coupling = 0.5 * (centre_k + shifted(cond_pad, spatial, along_dim, offset))
            running = running + coupling * (centre_v - shifted(field_pad, spatial, along_dim, offset))
    return running


def node_values(node_index):
    return jnp.cos(math.pi * node_index.astype(jnp.float32) / (NODES - 1))


def pair_mean(modes):
    return 0.5 * (modes[:, 0::2] + modes[:, 1::2])


def log_field(values, along_x, along_z, along_y):
    weighted = (along_x.T * values)[:, None, :] * along_z.T[None, :, :]
    flattened = weighted.reshape(weighted.shape[0] * weighted.shape[1], weighted.shape[2])
    product = jnp.dot(flattened, along_y, precision=lax.Precision.HIGHEST)
    return product.reshape(weighted.shape[0], weighted.shape[1], along_y.shape[1])


def restrict(tensor):
    blocks = tensor.reshape(tensor.shape[0] // 2, 2, tensor.shape[1] // 2, 2, tensor.shape[2] // 2, 2)
    return blocks.sum(axis=(1, 3, 5)) * 0.125


def solve_member(source, conduct):
    spatial = (0, 1, 2)
    cond_pad = jnp.pad(conduct, 1)
    diagonal = diagonal_of(cond_pad, spatial)
    update = source / (CENTRE * diagonal)
    result = update
    residual = source
    for keep_part, push_part in sweep_factors(SWEEPS):
        residual = residual - apply_op(jnp.pad(update, 1), cond_pad, spatial)
        update = keep_part * update + push_part * residual / diagonal
        result = result + update
    return result


def reference(node_fine, node_coarse, weight_fine, weight_coarse, mode_x, mode_y, mode_z, source_fine, source_coarse):
    mode_xc = pair_mean(mode_x)
    mode_yc = pair_mean(mode_y)
    mode_zc = pair_mean(mode_z)

    def fine_step(running, member_item):
        node_index, weight = member_item
        conduct = jnp.exp(log_field(node_values(node_index), mode_x, mode_z, mode_y))
        solved = solve_member(source_fine, conduct)
        return running + weight.astype(jnp.float32) * restrict(solved), None

    def coarse_step(running, member_item):
        node_index, weight = member_item
        conduct = jnp.exp(log_field(node_values(node_index), mode_xc, mode_zc, mode_yc))
        solved = solve_member(source_coarse, conduct)
        return running + weight.astype(jnp.float32) * solved, None

    running = jnp.zeros((NXC, NZC, NYC), jnp.float32)
    running, ignored = lax.scan(fine_step, running, (node_fine, weight_fine))
    running, ignored = lax.scan(coarse_step, running, (node_coarse, weight_coarse))
    return running
```

```python
import math

import jax
import jax.numpy as jnp
import numpy as np
from jax import lax
from jax.experimental import pallas as pl
from jax.experimental.pallas import tpu as pltpu
from jax.sharding import PartitionSpec as P

NODES = 9
SWEEPS = 3
CENTRE = 1.125
HALF_WIDTH = 0.875
SPREAD_RATIO = CENTRE / HALF_WIDTH

LANES = 128
HALO = SWEEPS
EDGE = 4
PAD = 8
FAR = -2048.0


def sweep_factors(sweep_count):
    previous = 1.0 / SPREAD_RATIO
    factors = []
    for _ in range(sweep_count - 1):
        current = 1.0 / (2.0 * SPREAD_RATIO - previous)
        factors.append((current * previous, 2.0 * current / HALF_WIDTH))
        previous = current
    return factors


(A1, B1), (A2, B2) = sweep_factors(SWEEPS)
FIRST = (A1 + (CENTRE - 1.0) * B1) / B1
KEEP0 = (1.0 - B2 * A1 / B1) / (B1 * B2)
KEEP1 = (1.0 + A2 + B2 / B1 - B2) / B2
SCALE = 2.0 / CENTRE * B1 * B2


def pieces(value):
    high = value.astype(jnp.bfloat16)
    rest = value - high.astype(jnp.float32)
    mid = rest.astype(jnp.bfloat16)
    low = (rest - mid.astype(jnp.float32)).astype(jnp.bfloat16)
    return high, mid, low


def outer_pieces(value):
    high = lax.reduce_precision(value, 8, 7)
    rest = value - high
    mid = lax.reduce_precision(rest, 8, 7)
    low = lax.reduce_precision(rest - mid, 8, 7)
    return tuple(part.astype(jnp.bfloat16) for part in (high, mid, low))


def smooth_kernel(
    groups, nx, ny, nz, pair,
    par_ref, sel_ref, zt_ref, xb_ref, yt_ref, src_ref, spread_ref, ym_ref, rt_ref, xin_ref,
    out_ref,
    yz_ref, c_ref, kz_ref, q_ref, d_ref, e_ref, u_ref,
):
    height = ny + 2 * EDGE
    lane = lax.broadcasted_iota(jnp.int32, (height, LANES), 1) % nz
    is_last = lane == nz - 1
    is_first = lane == 0
    mid = pl.ds(PAD, height)
    up = pl.ds(PAD + 1, height)
    down = pl.ds(PAD - 1, height)

    named = lax.dot_general(
        par_ref[...], sel_ref[...], (((0,), (0,)), ((), ())),
        precision=lax.Precision.HIGHEST, preferred_element_type=jnp.float32,
    )
    weights = []
    for g in range(groups):
        block = named[:, g * LANES:(g + 1) * LANES]
        yz_ref[g] = block * zt_ref[...]
        weights.append(block[14:15, :])

    def conduct(i, carry):
        row = xb_ref[i]
        for g in range(groups):
            high, middle, low = pieces(row * yz_ref[g])
            stacked = jnp.concatenate([high, middle, low, high, middle, high], axis=0)
            power = jnp.dot(yt_ref[...], stacked, preferred_element_type=jnp.float32)
            c_ref[g, i, mid, :] = jnp.exp(power)
        return carry

    lax.fori_loop(0, nx + 2 * HALO, conduct, 0)

    def start(i, carry):
        source = jnp.concatenate(pieces(src_ref[i - 1]), axis=0)
        force = lax.dot_general(
            source, spread_ref[...], (((0,), (0,)), ((), ())),
            preferred_element_type=jnp.float32,
        )
        mask = ym_ref[...] * xin_ref[i]
        for g in range(groups):
            c0 = c_ref[g, i, mid, :]
            zp = jnp.where(is_last, 0.0, pltpu.roll(c0, LANES - 1, 1))
            zm = jnp.where(is_first, 0.0, pltpu.roll(c0, 1, 1))
            total = (
                6.0 * c0 + (c_ref[g, i - 1, mid, :] + c_ref[g, i + 1, mid, :])
                + (c_ref[g, i, up, :] + c_ref[g, i, down, :]) + (zp + zm)
            )
            q = mask / (total + 1e-30)
            q_ref[g, i, mid, :] = q
            d_ref[g, i, mid, :] = force * q
            kz_ref[g, i, mid, :] = jnp.where(is_last, 0.0, c0 + zp)
        return carry

    lax.fori_loop(1, nx + 2 * HALO - 1, start, 0)

    def around(g, i, v_ref, mid, up, down):
        c0 = c_ref[g, i, mid, :]
        v0 = v_ref[g, i, mid, :]
        kz = kz_ref[g, i, mid, :]
        near = (c0 + c_ref[g, i + 1, mid, :]) * v_ref[g, i + 1, mid, :]
        near += (c0 + c_ref[g, i - 1, mid, :]) * v_ref[g, i - 1, mid, :]
        near += (c0 + c_ref[g, i, up, :]) * v_ref[g, i, up, :]
        near += (c0 + c_ref[g, i, down, :]) * v_ref[g, i, down, :]
        near += kz * pltpu.roll(v0, LANES - 1, 1)
        near += pltpu.roll(kz * v0, 1, 1)
        return v0, q_ref[g, i, mid, :] * near

    def first(i, carry):
        for g in range(groups):
            v0, near = around(g, i, d_ref, mid, up, down)
            e_ref[g, i, mid, :] = FIRST * v0 + near
        return carry

    lax.fori_loop(2, nx + 2 * HALO - 2, first, 0)

    inner = pl.ds(PAD + EDGE, ny)
    inner_up = pl.ds(PAD + EDGE + 1, ny)
    inner_down = pl.ds(PAD + EDGE - 1, ny)
    step = 2 if pair else 1
    scale = SCALE * (0.125 if pair else 1.0)

    def second(k, carry):
        total = None
        for s in range(step):
            i = HALO + step * k + s
            for g in range(groups):
                v0, near = around(g, i, e_ref, inner, inner_up, inner_down)
                u = KEEP0 * d_ref[g, i, inner, :] + KEEP1 * v0 + near
                u = u * (scale * weights[g])
                total = u if total is None else total + u
        u_ref[...] = total
        if pair:
            total = u_ref[pl.ds(0, ny // 2, stride=2), :] + u_ref[pl.ds(1, ny // 2, stride=2), :]
        stacked = jnp.concatenate(pieces(total), axis=1)
        out_ref[k] = lax.dot_general(
            rt_ref[...], stacked, (((1,), (1,)), ((), ())),
            preferred_element_type=jnp.float32,
        )
        return carry

    lax.fori_loop(0, nx // step, second, 0)


def smooth(par, sel, zt, xb, yt, src, ym, xin, nx, ny, nz, pair):
    groups = sel.shape[1] // LANES
    height = ny + 2 * EDGE
    members = LANES // nz
    spread = np.tile(np.eye(nz, dtype=np.float32), (3, members))
    out_z = nz // 2 if pair else nz
    rt = np.tile(np.eye(out_z, dtype=np.float32).repeat(nz // out_z, axis=1), (1, 3 * members))
    vmem = pl.BlockSpec(memory_space=pltpu.VMEM)
    smem = pl.BlockSpec(memory_space=pltpu.SMEM)
    nxe = nx + 2 * HALO
    grid = pltpu.VMEM((groups, nxe, height + 2 * PAD, LANES), jnp.float32)

    def kernel(*refs):
        smooth_kernel(groups, nx, ny, nz, pair, *refs)

    step = 2 if pair else 1
    return pl.pallas_call(
        kernel,
        out_shape=jax.ShapeDtypeStruct((nx // step, out_z, ny // step), jnp.float32),
        in_specs=[vmem] * 9 + [smem],
        out_specs=vmem,
        scratch_shapes=[pltpu.VMEM((groups, 16, LANES), jnp.float32), grid, grid, grid, grid, grid,
                        pltpu.VMEM((ny, LANES), jnp.float32)],
        compiler_params=pltpu.CompilerParams(vmem_limit_bytes=60 << 20),
        name="fine_smooth" if pair else "coarse_smooth",
    )(par, sel, zt, xb, yt, src, jnp.asarray(spread, jnp.bfloat16), ym,
      jnp.asarray(rt, jnp.bfloat16), xin)


def selector(devices, block, first_row, per_device, nz):
    members = devices * per_device
    out = np.zeros((devices * block, members * nz), np.float32)
    for k in range(members):
        row = (k // per_device) * block + first_row + k % per_device
        out[row, k * nz:(k + 1) * nz] = 1.0
    return out


def tables(mode_x, mode_y, mode_z, x0, nx, y0, ny, nz):
    terms = mode_x.shape[0]
    nxe, height = nx + 2 * HALO, ny + 2 * EDGE
    px = jnp.pad(mode_x, ((0, 0), (HALO, HALO)))
    px = lax.dynamic_slice_in_dim(px, x0, nxe, 1)
    gx = x0 - HALO + jnp.arange(nxe, dtype=jnp.int32)
    x_in = ((gx >= 0) & (gx < mode_x.shape[1])).astype(jnp.float32)
    xcol = jnp.concatenate(
        [px.T, jnp.ones((nxe, 1), jnp.float32), ((1.0 - x_in) * FAR)[:, None],
         jnp.zeros((nxe, 2), jnp.float32)], axis=1)
    xb = jnp.broadcast_to(xcol[:, :, None], (nxe, terms + 4, LANES))
    py = jnp.pad(mode_y, ((0, 0), (EDGE, EDGE)))
    py = lax.dynamic_slice_in_dim(py, y0, height, 1)
    gy = y0 - EDGE + jnp.arange(height, dtype=jnp.int32)
    y_in = ((gy >= 0) & (gy < mode_y.shape[1])).astype(jnp.float32)
    ycol = jnp.concatenate(
        [py.T, ((1.0 - y_in) * FAR)[:, None], jnp.ones((height, 1), jnp.float32),
         jnp.zeros((height, 2), jnp.float32)], axis=1)
    high, middle, low = outer_pieces(ycol)
    yt = jnp.concatenate([high, high, high, middle, middle, low], axis=1)
    ym = jnp.broadcast_to(y_in[:, None], (height, LANES))
    zt = jnp.concatenate(
        [jnp.tile(mode_z, (1, LANES // nz)), jnp.ones((2, LANES), jnp.float32),
         jnp.zeros((2, LANES), jnp.float32)], axis=0)
    return zt, xb, yt, ym, x_in


def pair_mean(modes):
    return 0.5 * (modes[:, 0::2] + modes[:, 1::2])


def solution(mesh):
    members, tiles = mesh.shape["member"], mesh.shape["tile"]
    per_strip = members // tiles
    assert per_strip == 2 and members == tiles * per_strip and tiles >= 4
    axes = ("member", "tile")

    def flat(b, a, t):
        return (b * per_strip + a) * tiles + t

    def quarter(b, t):
        return b ^ t ^ jnp.where(t < tiles // 2, tiles - 1, 0)

    def quarter_py(b, t):
        return b ^ t ^ (tiles - 1 if t < tiles // 2 else 0)

    def chain(bit, sign):
        pairs = []
        for b in range(tiles):
            for t in range(tiles):
                for a, move in ((0, sign), (1, -sign)):
                    to = t + move
                    if 0 <= to < tiles:
                        pairs.append((flat(b, a, t), flat(b ^ bit, a, to)))
                    else:
                        pairs.append((flat(b, a, t), flat(b ^ bit, 1 - a, t)))
        return pairs

    def receiver(b, a, t, bit, sign):
        to = t + jnp.where(a == 0, sign, -sign)
        ok = (to >= 0) & (to < tiles)
        return b ^ bit, jnp.where(ok, a, 1 - a), jnp.where(ok, to, t)

    def body(node_fine, node_coarse, weight_fine, weight_coarse, mode_x, mode_y, mode_z,
             source_fine, source_coarse):
        m, t = lax.axis_index("member"), lax.axis_index("tile")
        a, b = m % per_strip, m // per_strip
        terms = mode_x.shape[0]
        strip, nz, _ = source_fine.shape
        nx = mode_x.shape[1] // members
        ny = mode_y.shape[1] // tiles
        cx, cz, cy = source_coarse.shape[0] // members, source_coarse.shape[1], source_coarse.shape[2]
        reach = SWEEPS - 1
        height = ny + 2 * EDGE
        n_fine, n_coarse = node_fine.shape[0], node_coarse.shape[0]
        block = -(-(n_fine + n_coarse) // 8) * 8

        nodes = jnp.concatenate([node_fine, node_coarse], axis=0)
        values = jnp.cos(math.pi * nodes.astype(jnp.float32) / (NODES - 1))
        weight = jnp.concatenate([weight_fine, weight_coarse]).astype(jnp.float32)[:, None]
        par = jnp.concatenate(
            [values, jnp.ones((n_fine + n_coarse, 2), jnp.float32), weight,
             jnp.zeros((n_fine + n_coarse, 1), jnp.float32)], axis=1)
        width = terms + 4
        par = jnp.pad(par, ((0, block - par.shape[0]), (0, LANES - width)))

        near = lax.ppermute(par, "member", [(i, i ^ 1) for i in range(members)])
        par = jnp.concatenate([par, near], axis=0)

        fine_wide = jnp.pad(source_fine, ((0, 0), (0, 0), (EDGE, EDGE)))
        coarse_wide = jnp.pad(source_coarse, ((reach, reach), (0, 0), (0, 0)))

        def coarse_rows(bit, sign):
            rb, ra, _ = receiver(b, a, t, bit, sign)
            low_side = jnp.where(a == 0, sign, -sign) < 0
            rows = lax.dynamic_slice(
                coarse_wide, (cx * (rb * per_strip + ra), 0, jnp.where(low_side, 0, cy - reach)),
                (cx + 2 * reach, cz, reach))
            return rows.transpose(2, 0, 1).reshape(reach, -1)

        bits = []
        bit = tiles // 2
        while bit:
            bits.append(bit)
            bit //= 2
        rb, ra, rt = receiver(b, a, t, bits[0], 1)
        planes = lax.dynamic_slice(
            fine_wide, (jnp.where(a == 0, strip - reach, 0), 0, ny * quarter(rb, rt)),
            (reach, nz, height)).reshape(reach * nz, height)
        edge = coarse_rows(bits[0], 1)
        count, rows = par.shape[0], edge.shape[0]
        wide = max(height, LANES, edge.shape[1])
        sent = jnp.concatenate(
            [jnp.pad(part, ((0, 0), (0, wide - part.shape[1]))) for part in (planes, par, edge)],
            axis=0)
        got = lax.ppermute(sent, axes, chain(bits[0], 1))
        planes = got[:reach * nz, :height].reshape(reach, nz, height)
        par = jnp.concatenate([par, got[reach * nz:reach * nz + count, :LANES]], axis=0)
        edge_one = got[reach * nz + count:, :edge.shape[1]]
        edge = coarse_rows(bits[1], -1)
        count = par.shape[0]
        got = lax.ppermute(jnp.concatenate([par, edge], axis=0), axes, chain(bits[1], -1))
        par = jnp.concatenate([par, got[:count]], axis=0)
        edge_two = got[count:]
        for bit in bits[2:]:
            got = lax.ppermute(par, "member", [(i, i ^ (bit * per_strip)) for i in range(members)])
            par = jnp.concatenate([par, got], axis=0)
        par = par[:, :width]

        q = quarter(b, t)
        own = lax.dynamic_slice(
            fine_wide, (jnp.where(a == 0, 0, strip - nx - reach), 0, ny * q), (nx + reach, nz, height))
        src = jnp.where(a == 0, jnp.concatenate([planes, own], axis=0),
                        jnp.concatenate([own, planes], axis=0))
        zt, xb, yt, ym, x_in = tables(
            mode_x, mode_y, mode_z, t * strip + a * nx, nx, q * ny, ny, nz)
        sel = jnp.asarray(selector(members, block, 0, n_fine, nz))
        fine = smooth(par, sel, zt, xb, yt, src, ym, x_in, nx, ny, nz, True)
        pairs = [(flat(b_, a_, t_), flat(t_, a_, quarter_py(b_, t_)))
                 for b_ in range(tiles) for a_ in range(per_strip) for t_ in range(tiles)]
        arrived = lax.ppermute(fine, axes, pairs)

        own = lax.dynamic_slice_in_dim(coarse_wide, cx * m, cx + 2 * reach, 0)

        def unpack(edge):
            return edge.reshape(reach, cx + 2 * reach, cz).transpose(1, 2, 0)

        low = unpack(jnp.where(a == 0, edge_one, edge_two))
        high = unpack(jnp.where(a == 0, edge_two, edge_one))
        gap = jnp.zeros(own.shape[:2] + (EDGE - reach,), jnp.float32)
        src = jnp.concatenate([gap, low, own, high, gap], axis=2)
        zt, xb, yt, ym, x_in = tables(
            pair_mean(mode_x), pair_mean(mode_y), pair_mean(mode_z), cx * m, cx, t * cy, cy, cz)
        sel = jnp.asarray(selector(members, block, n_fine, n_coarse, cz))
        coarse = smooth(par, sel, zt, xb, yt, src, ym, x_in, cx, cy, cz, False)
        return arrived + coarse

    return jax.shard_map(
        body,
        mesh=mesh,
        in_specs=(
            P("member", None), P("member", None), P("member"), P("member"),
            P(), P(), P(), P("tile", None, None), P(None, None, "tile"),
        ),
        out_specs=P("member", None, "tile"),
        check_vma=False,
    )
```

```python
import functools
import math

import jax
import jax.numpy as jnp
from jax import lax
from jax.experimental import pallas as pl
from jax.experimental.pallas import tpu as pltpu
from jax.sharding import PartitionSpec as P

NODES = 9
SWEEPS = 3
CENTRE = 1.125
HALF_WIDTH = 0.875
SPREAD_RATIO = CENTRE / HALF_WIDTH

LANES = 128
HALO = SWEEPS
REACH = SWEEPS - 1
EDGE = 4
PAD = 8
FAR = -2048.0
TERMS = 16
BLOCK = 8
UNROLL = (2, 2, 2, 2)


def sweep_factors(sweep_count):
    previous = 1.0 / SPREAD_RATIO
    factors = []
    for _ in range(sweep_count - 1):
        current = 1.0 / (2.0 * SPREAD_RATIO - previous)
        factors.append((current * previous, 2.0 * current / HALF_WIDTH))
        previous = current
    return factors


(A1, B1), (A2, B2) = sweep_factors(SWEEPS)
FIRST = A1 / B1 + CENTRE - 1.0
KEEP0 = (1.0 - B2 * A1 / B1) / (B1 * B2)
KEEP1 = (1.0 + A2 + B2 / B1 - B2) / B2
SHIFT = 0.5 * (FIRST + KEEP1)
REST = KEEP0 + KEEP1 * FIRST - SHIFT * SHIFT
SCALE = 2.0 / CENTRE * B1 * B2 * SHIFT ** 3
EXACT = lax.Precision.HIGHEST
ROWS = (((0,), (0,)), ((), ()))
COLUMNS = (((1,), (1,)), ((), ()))


def iota(shape, dim):
    return lax.broadcasted_iota(jnp.int32, shape, dim)


def pieces(value):
    high = value.astype(jnp.bfloat16)
    rest = value - high.astype(jnp.float32)
    mid = rest.astype(jnp.bfloat16)
    low = (rest - mid.astype(jnp.float32)).astype(jnp.bfloat16)
    return high, mid, low


def aligned(at):
    return at if isinstance(at, int) else pl.multiple_of(at, 8)


def quarter(b, t, tiles):
    return b ^ t ^ jnp.where(t < tiles // 2, tiles - 1, 0)


class Place:
    def __init__(self, tiles):
        m, t = lax.axis_index("member"), lax.axis_index("tile")
        self.tiles, self.m, self.t = tiles, m, t
        self.a, self.b = m % 2, m // 2
        self.half = self.a ^ (t % 2)

    def beside(self, outward):
        step = jnp.where(self.half == 1, 1, -1)
        to = self.t + (step if outward else -step)
        return jnp.where((to >= 0) & (to < self.tiles), to, self.t)


def prep_kernel(tiles, nx, ny, cx, bits, nf_ref, nc_ref, wf_ref, wc_ref, sf_ref, sc_ref,
                a_ref, b_ref, par_ref, plane_ref, sem):
    here = Place(tiles)
    strip, nz, full_y = sf_ref.shape
    full_x, cz, cy = sc_ref.shape
    height = ny + 2 * EDGE
    start = jnp.where(here.half == 1, strip - REACH, 0)
    copy = pltpu.make_async_copy(sf_ref.at[pl.ds(start, REACH)], plane_ref, sem)
    copy.start()

    def node_values(ref):
        nodes = ref[...]
        out = jnp.zeros(nodes.shape, jnp.float32)
        for k in range(NODES):
            out = jnp.where(nodes == k, math.cos(math.pi * k / (NODES - 1)), out)
        return out

    n_fine, terms = nf_ref.shape
    n_coarse = nc_ref.shape[0]
    row, lane = iota((BLOCK, LANES), 0), iota((BLOCK, LANES), 1)
    base = jnp.where((lane == terms) | (lane == terms + 1), 1.0, 0.0)
    for k in range(n_fine + n_coarse):
        weight = wf_ref[k] if k < n_fine else wc_ref[k - n_fine]
        base = jnp.where((row == k) & (lane == terms + 2), weight.astype(jnp.float32), base)
    par_ref[...] = base
    par_ref[0:n_fine, 0:terms] = node_values(nf_ref)
    par_ref[n_fine:n_fine + n_coarse, 0:terms] = node_values(nc_ref)

    rows = REACH * nz
    per_group = rows // cz
    spot = iota((rows, LANES), 1)

    def coarse_side(to_b, last, at):
        first = cx * (to_b * 2 + here.a) - REACH
        total = jnp.zeros((rows, LANES), jnp.float32)
        for group in range((cx + 2 * REACH) // per_group):
            parts = [sc_ref[jnp.clip(first + group * per_group + k, 0, full_x - 1)]
                     for k in range(per_group)]
            block = jnp.concatenate(parts, axis=0)
            block = jnp.concatenate([block] * (LANES // cy), axis=1)
            to = at + REACH * group
            shift = jnp.where(last, (to - cy + REACH) % LANES, to % LANES)
            block = pltpu.roll(block, shift, 1)
            total = jnp.where((spot >= to) & (spot < to + REACH), block, total)
        return total

    b_ref[0:rows, :] = coarse_side(here.b ^ bits[1], here.half == 0, EDGE * 2)
    edge = coarse_side(here.b ^ bits[0], here.half == 1, height % LANES)
    b_ref[rows:rows + BLOCK, :] = par_ref[...]
    a_ref[rows:rows + BLOCK, 0:LANES] = par_ref[...]

    target = quarter(here.b ^ bits[0], here.beside(True), tiles)
    shift = (EDGE + full_y - ny * target) % full_y
    copy.wait()
    for k in range(REACH):
        turned = pltpu.roll(plane_ref[k], shift, 1)
        part = slice(k * nz, (k + 1) * nz)
        for col in range(a_ref.shape[1] // LANES):
            block = turned[:, col * LANES:(col + 1) * LANES]
            if col == height // LANES:
                block = jnp.where(iota((nz, LANES), 1) < height % LANES, block, edge[part])
            a_ref[part, col * LANES:(col + 1) * LANES] = block


def factors(ratio, terms, nx, ny, nz, x0, y0, full_x, full_y, tx_ref, ty_ref,
            xb_ref, yt_ref, zt_ref):
    nxe, height = nx + 2 * HALO, ny + 2 * EDGE
    row = iota((TERMS, LANES), 0)
    xw = pltpu.roll(tx_ref[0], (ratio * (HALO - x0) + 2 * LANES) % LANES, 1)
    if ratio == 2:
        xw = 0.5 * (xw + pltpu.roll(xw, LANES - 1, 1))
    for i in range(nxe):
        at = x0 - HALO + i
        far = jnp.where((at < 0) | (at >= full_x), FAR, 0.0)
        col = jnp.broadcast_to(xw[:, ratio * i:ratio * i + 1], (TERMS, LANES))
        xb_ref[i] = jnp.where(row == terms, 1.0, jnp.where(row == terms + 1, far, col))
    span = -(-ratio * height // LANES) * LANES
    yw = pltpu.roll(ty_ref[...], (ratio * (EDGE - y0) + ratio * full_y) % (ratio * full_y), 1)
    yw = jnp.concatenate([yw[:, :span]] * 6, axis=0)
    pick = jnp.where(iota((height, span), 1) // ratio == iota((height, span), 0), 1.0 / ratio, 0.0)
    yt = lax.dot_general(pick, yw, COLUMNS, precision=EXACT, preferred_element_type=jnp.float32)
    lane = iota(yt.shape, 1)
    at = y0 - EDGE + iota(yt.shape, 0)
    far = jnp.where((at < 0) | (at >= full_y), FAR, 0.0)
    yt = jnp.where(lane % TERMS == terms, far, jnp.where(lane % TERMS == terms + 1, 1.0, yt))
    high, mid, low = (part.astype(jnp.float32) for part in pieces(yt))
    yt_ref[...] = jnp.where(lane < 3 * TERMS, high, jnp.where(lane < 5 * TERMS, mid, low)).astype(
        jnp.bfloat16)
    down, across = iota((LANES, LANES), 0), iota((LANES, LANES), 1)
    pick = jnp.where(down // ratio == across % nz, 1.0 / ratio, 0.0)
    zt = jnp.dot(tx_ref[1], pick, precision=EXACT, preferred_element_type=jnp.float32)
    zt_ref[...] = jnp.where((row == terms) | (row == terms + 1), 1.0, zt)


def members_of(pars, groups, nz, first_row, per_device, zt_ref, yz_ref):
    weights = []
    for par_ref in pars:
        size = par_ref.shape[0]
        for g in range(groups):
            member = (LANES // nz) * g + iota((size, LANES), 1) // nz
            source = BLOCK * (member // per_device) + first_row + member % per_device
            pick = jnp.where(iota((size, LANES), 0) == source, 1.0, 0.0)
            named = lax.dot_general(par_ref[:, 0:TERMS], pick, ROWS, precision=EXACT,
                                    preferred_element_type=jnp.float32)
            yz_ref[len(weights)] = named * zt_ref[...]
            weights.append(named[TERMS - 2:TERMS - 1, :])
    return weights


def chunks(count, size, run):
    def step(j, carry):
        for s in range(size):
            run(size * j + s)
        return carry

    whole = count // size
    lax.fori_loop(0, whole, step, 0)
    for k in range(whole * size, count):
        run(k)


def sweeps(groups, nx, ny, nz, x0, y0, full_x, full_y, pair, weights,
           xb_ref, yt_ref, yz_ref, force, c_ref, kz_ref, q_ref, d_ref, e_ref, u_ref, finish):
    nxe, height = nx + 2 * HALO, ny + 2 * EDGE

    def conduct(i, carry):
        row = xb_ref[i]
        for g in range(groups):
            high, middle, low = pieces(row * yz_ref[g])
            stacked = jnp.concatenate([high, middle, low, high, middle, high], axis=0)
            power = jnp.dot(yt_ref[...], stacked, preferred_element_type=jnp.float32)
            c_ref[g, i, pl.ds(PAD, height), :] = jnp.exp(power)
        return carry

    lax.fori_loop(0, nxe, conduct, 0, unroll=UNROLL[0])

    lane = iota((8, LANES), 1) % nz
    is_last, is_first = lane == nz - 1, lane == 0

    def start(k):
        at = aligned(PAD + 8 * k)
        here, up, down = pl.ds(at, 8), pl.ds(at + 1, 8), pl.ds(at - 1, 8)
        own = pl.ds(aligned(8 * k), 8)
        for g in range(groups):
            before, c0 = c_ref[g, 0, here, :], c_ref[g, 1, here, :]
            for i in range(1, nxe - 1):
                after = c_ref[g, i + 1, here, :]
                zp = jnp.where(is_last, 0.0, pltpu.roll(c0, LANES - 1, 1))
                zm = jnp.where(is_first, 0.0, pltpu.roll(c0, 1, 1))
                total = (6.0 * c0 + (before + after)) + (
                    (c_ref[g, i, up, :] + c_ref[g, i, down, :]) + (zp + zm))
                q = (1.0 / SHIFT) / total
                q_ref[g, i, here, :] = q
                d_ref[g, i, here, :] = force(i - 1, own) * q
                kz_ref[g, i, here, :] = jnp.where(is_last, 0.0, c0 + zp)
                before, c0 = c0, after

    chunks(height // 8, UNROLL[1], start)

    def clear_planes(planes):
        for g in range(groups):
            for i in planes:
                zero = jnp.zeros((height, LANES), jnp.float32)
                q_ref[g, i, pl.ds(PAD, height), :] = zero
                d_ref[g, i, pl.ds(PAD, height), :] = zero

    def clear_rows(at):
        for g in range(groups):
            for i in range(1, nxe - 1):
                zero = jnp.zeros((EDGE, LANES), jnp.float32)
                q_ref[g, i, pl.ds(PAD + at, EDGE), :] = zero
                d_ref[g, i, pl.ds(PAD + at, EDGE), :] = zero

    pl.when(x0 == 0)(lambda: clear_planes(range(1, HALO)))
    pl.when(x0 + nx == full_x)(lambda: clear_planes(range(nx + HALO, nxe - 1)))
    pl.when(y0 == 0)(lambda: clear_rows(0))
    pl.when(y0 + ny == full_y)(lambda: clear_rows(EDGE + ny))

    def walk(g, v_ref, first, last, here, up, down):
        c0, v0 = c_ref[g, first, here, :], v_ref[g, first, here, :]
        v_before = v_ref[g, first - 1, here, :]
        k_before = c_ref[g, first - 1, here, :] + c0
        for i in range(first, last):
            c_after, v_after = c_ref[g, i + 1, here, :], v_ref[g, i + 1, here, :]
            k_after = c0 + c_after
            kz = kz_ref[g, i, here, :]
            along_x = k_after * v_after + k_before * v_before
            along_y = ((c0 + c_ref[g, i, up, :]) * v_ref[g, i, up, :]
                       + (c0 + c_ref[g, i, down, :]) * v_ref[g, i, down, :])
            along_z = kz * pltpu.roll(v0, LANES - 1, 1) + pltpu.roll(kz * v0, 1, 1)
            yield i, v0 + q_ref[g, i, here, :] * ((along_x + along_y) + along_z)
            c0, v0, v_before, k_before = c_after, v_after, v0, k_after

    def first(k):
        at = aligned(PAD + 8 * k)
        here, up, down = pl.ds(at, 8), pl.ds(at + 1, 8), pl.ds(at - 1, 8)
        for g in range(groups):
            for i, value in walk(g, d_ref, 2, nxe - 2, here, up, down):
                e_ref[g, i, here, :] = value

    chunks(height // 8, UNROLL[2], first)

    step = 2 if pair else 1
    scale = SCALE * (0.125 if pair else 1.0)
    keep = REST / (SHIFT * SHIFT)

    def second(k):
        at = PAD + EDGE + 8 * k
        here, up, down = pl.ds(at, 8), pl.ds(at + 1, 8), pl.ds(at - 1, 8)
        out = [None] * (nx // step)
        for g in range(groups):
            gain = jnp.broadcast_to(scale * weights[g], (8, LANES))
            held = None
            for i, value in walk(g, e_ref, HALO, nx + HALO, here, up, down):
                value = value + keep * d_ref[g, i, here, :]
                j = i - HALO
                if j % step:
                    value = held + value
                held = value
                if j % step == step - 1:
                    value = gain * value
                    out[j // step] = value if g == 0 else out[j // step] + value
        for j, value in enumerate(out):
            u_ref[j, pl.ds(aligned(8 * k), 8), :] = value

    chunks(ny // 8, UNROLL[3], second)

    out_z = nz // step
    match = iota((out_z, 3 * LANES), 1) % nz // step == iota((out_z, 3 * LANES), 0)
    gather = jnp.where(match, 1.0, 0.0).astype(jnp.bfloat16)
    for j in range(nx // step):
        if pair:
            total = (u_ref[j, pl.ds(0, ny // 2, stride=2), :]
                     + u_ref[j, pl.ds(1, ny // 2, stride=2), :])
        else:
            total = u_ref[j]
        stacked = jnp.concatenate(pieces(total), axis=1)
        finish(j, lax.dot_general(gather, stacked, COLUMNS, preferred_element_type=jnp.float32))


def spread_of(nz):
    match = iota((3 * nz, LANES), 0) % nz == iota((3 * nz, LANES), 1) % nz
    return jnp.where(match, 1.0, 0.0).astype(jnp.bfloat16)


def force_of(source, spread):
    return lax.dot_general(jnp.concatenate(pieces(source), axis=0), spread, ROWS,
                           preferred_element_type=jnp.float32)


def fine_place(here, strip, nx, ny):
    return here.t * strip + here.half * nx, quarter(here.b, here.t, here.tiles) * ny


def table_kernel(tiles, fine_sizes, coarse_sizes, mx_ref, my_ref, mz_ref, sf_ref, sc_ref, order_ref,
                 fx_ref, fy_ref, fz_ref, ff_ref, cx_ref, cy_ref, cz_ref, cf_ref,
                 tx_ref, ty_ref, own_ref, sem):
    here = Place(tiles)
    nx, ny, nz, full_x, full_y = fine_sizes
    strip = sf_ref.shape[0]
    count = nx + REACH
    copy = pltpu.make_async_copy(
        sf_ref.at[pl.ds(jnp.where(here.half == 0, 0, strip - count), count)], own_ref, sem)
    copy.start()
    terms = mx_ref.shape[0]
    tx_ref[...] = jnp.zeros_like(tx_ref)
    tx_ref[0, 0:terms, 0:mx_ref.shape[1]] = mx_ref[...]
    tx_ref[1, 0:terms, 0:mz_ref.shape[1]] = mz_ref[...]
    ty_ref[...] = jnp.zeros_like(ty_ref)
    ty_ref[0:terms, :] = my_ref[...]
    x0, y0 = fine_place(here, strip, nx, ny)
    factors(1, terms, nx, ny, nz, x0, y0, full_x, full_y, tx_ref, ty_ref, fx_ref, fy_ref, fz_ref)
    shift = (EDGE + full_y - y0) % full_y

    nx, ny, nz, full_x, full_y = coarse_sizes
    x0 = here.m * nx
    factors(2, terms, nx, ny, nz, x0, here.t * ny, full_x, full_y, tx_ref, ty_ref,
            cx_ref, cy_ref, cz_ref)
    spread = spread_of(nz)
    for k in range(nx + 2 * REACH):
        x = jnp.clip(x0 - REACH + k, 0, full_x - 1)
        cf_ref[k] = jnp.zeros_like(cf_ref[k])
        cf_ref[k, EDGE:EDGE + ny, :] = force_of(sc_ref[x], spread)

    copy.wait()
    height = ff_ref.shape[1]
    spread = spread_of(fine_sizes[2])

    def place(k):
        source = pltpu.roll(own_ref[k], shift, 1)[:, :height]
        ff_ref[k + REACH * (1 - here.half)] = force_of(source, spread)

    chunks(count, 5 if count % 5 == 0 else 2, place)


def fine_kernel(tiles, groups, sizes, strip, per_device,
                x_ref, y_ref, z_ref, f_ref, one_ref, two_ref, side_ref, order_ref, out_ref,
                yz_ref, c_ref, kz_ref, q_ref, d_ref, e_ref, u_ref, edge_ref):
    here = Place(tiles)
    nx, ny, nz, full_x, full_y = sizes
    height = ny + 2 * EDGE
    x0, y0 = fine_place(here, strip, nx, ny)
    weights = members_of((one_ref, two_ref), groups, nz, 0, per_device, z_ref, yz_ref)
    spread = spread_of(nz)
    for k in range(REACH):
        edge_ref[k] = force_of(side_ref[k * nz:(k + 1) * nz, :height], spread)
    count = nx + REACH

    def force(k, rows):
        if k < REACH:
            return jnp.where(here.half == 0, edge_ref[k, rows, :], f_ref[k, rows, :])
        if k >= count:
            return jnp.where(here.half == 0, f_ref[k, rows, :], edge_ref[k - count, rows, :])
        return f_ref[k, rows, :]

    def finish(j, value):
        out_ref[j] = value

    sweeps(2 * groups, nx, ny, nz, x0, y0, full_x, full_y, True, weights, x_ref, y_ref, yz_ref,
           force, c_ref, kz_ref, q_ref, d_ref, e_ref, u_ref, finish)


def coarse_kernel(tiles, groups, sizes, first_row, per_device,
                  x_ref, y_ref, z_ref, f_ref, par_ref, base_ref, out_ref,
                  yz_ref, c_ref, kz_ref, q_ref, d_ref, e_ref, u_ref):
    here = Place(tiles)
    nx, ny, nz, full_x, full_y = sizes
    weights = members_of((par_ref,), groups, nz, first_row, per_device, z_ref, yz_ref)

    def force(k, rows):
        return f_ref[k, rows, :]

    def finish(j, value):
        out_ref[j] = value if base_ref is None else base_ref[j] + value

    sweeps(groups, nx, ny, nz, here.m * nx, here.t * ny, full_x, full_y, False, weights, x_ref,
           y_ref, yz_ref, force, c_ref, kz_ref, q_ref, d_ref, e_ref, u_ref, finish)


def coarse_near_kernel(tiles, groups, sizes, first_row, per_device, side_at,
                       x_ref, y_ref, z_ref, f_ref, par_ref, a_ref, b_ref, out_ref, full_ref,
                       *scratch_refs):
    here = Place(tiles)
    nx, ny, nz, _, _ = sizes
    spread = spread_of(nz)
    per_group = side_at[2]
    for k in range(nx + 2 * REACH):
        full_ref[k] = f_ref[k]
        rows = slice(k % per_group * nz, (k % per_group + 1) * nz)
        found = []
        for ref, at in ((a_ref, side_at[0]), (b_ref, side_at[1])):
            low = at // 16 * 16
            block = force_of(ref[rows, low:low + 16], spread)
            at = at - low + REACH * (k // per_group)
            found.append(block[at:at + REACH])
        full_ref[k, EDGE - REACH:EDGE, :] = jnp.where(here.half == 0, found[0], found[1])
        full_ref[k, EDGE + ny:EDGE + ny + REACH, :] = jnp.where(
            here.half == 0, found[1], found[0])
    coarse_kernel(tiles, groups, sizes, first_row, per_device, x_ref, y_ref, z_ref, full_ref,
                  par_ref, None, out_ref, *scratch_refs)


def scratch(groups, nx, ny, count):
    nxe, height = nx + 2 * HALO, ny + 2 * EDGE
    grid = pltpu.VMEM((groups, nxe, height + 2 * PAD, LANES), jnp.float32)
    return [pltpu.VMEM((groups, TERMS, LANES), jnp.float32), grid, grid, grid, grid, grid,
            pltpu.VMEM((count, ny, LANES), jnp.float32)]


def level_shapes(nx, ny):
    nxe, height = nx + 2 * HALO, ny + 2 * EDGE
    return (jax.ShapeDtypeStruct((nxe, TERMS, LANES), jnp.float32),
            jax.ShapeDtypeStruct((height, 6 * TERMS), jnp.bfloat16),
            jax.ShapeDtypeStruct((TERMS, LANES), jnp.float32),
            jax.ShapeDtypeStruct((nx + 2 * REACH, height, LANES), jnp.float32))


def limit(mebibytes):
    return pltpu.CompilerParams(vmem_limit_bytes=mebibytes << 20)


VMEM = pl.BlockSpec(memory_space=pltpu.VMEM)
SMEM = pl.BlockSpec(memory_space=pltpu.SMEM)
HBM = pl.BlockSpec(memory_space=pl.ANY)


def solution(mesh):
    members, tiles = mesh.shape["member"], mesh.shape["tile"]
    assert members == 2 * tiles and tiles >= 4
    axes = ("member", "tile")
    bits = (tiles // 2, tiles // 4)
    others = [d for d in range(1, tiles) if d not in bits]

    def flat(b, a, t):
        return (b * 2 + a) * tiles + t

    def everywhere(rule):
        return [(flat(b, a, t), flat(*rule(b, a, t)))
                for b in range(tiles) for a in range(2) for t in range(tiles)]

    def beside(bit, outward):
        def rule(b, a, t):
            step = 1 if a ^ (t % 2) else -1
            to = t + (step if outward else -step)
            return b ^ bit, a, to if 0 <= to < tiles else t
        return everywhere(rule)

    def owner(b, a, t):
        return t, a ^ (t % 2), b ^ t ^ (tiles - 1 if t < tiles // 2 else 0)

    def body(node_fine, node_coarse, weight_fine, weight_coarse, mode_x, mode_y, mode_z,
             source_fine, source_coarse):
        strip, nz, full_y = source_fine.shape
        full_cx, cz, cy = source_coarse.shape
        full_x = mode_x.shape[1]
        nx, ny, cx = full_x // members, full_y // tiles, full_cx // members
        n_fine, n_coarse = node_fine.shape[0], node_coarse.shape[0]
        height = ny + 2 * EDGE
        rows = REACH * nz
        width = -(-(height + REACH * 2) // LANES) * LANES
        fine_sizes = nx, ny, nz, full_x, full_y
        coarse_sizes = cx, cy, cz, full_cx, cy * tiles

        side_a, side_b, par = pl.pallas_call(
            functools.partial(prep_kernel, tiles, nx, ny, cx, bits),
            out_shape=(jax.ShapeDtypeStruct((rows + BLOCK, width), jnp.float32),
                       jax.ShapeDtypeStruct((rows + BLOCK, LANES), jnp.float32),
                       jax.ShapeDtypeStruct((BLOCK, LANES), jnp.float32)),
            in_specs=[VMEM, VMEM, SMEM, SMEM, HBM, VMEM],
            out_specs=(VMEM, VMEM, VMEM),
            scratch_shapes=[pltpu.VMEM((REACH, nz, full_y), jnp.float32), pltpu.SemaphoreType.DMA],
            compiler_params=limit(4),
            name="prep",
        )(node_fine, node_coarse, weight_fine, weight_coarse, source_fine, source_coarse)

        made = pl.pallas_call(
            functools.partial(table_kernel, tiles, fine_sizes, coarse_sizes),
            out_shape=level_shapes(nx, ny) + level_shapes(cx, cy),
            in_specs=[VMEM] * 3 + [HBM, VMEM, HBM],
            out_specs=(VMEM,) * 8,
            scratch_shapes=[pltpu.VMEM((2, TERMS, LANES), jnp.float32),
                            pltpu.VMEM((TERMS, full_y), jnp.float32),
                            pltpu.VMEM((nx + REACH, nz, full_y), jnp.float32),
                            pltpu.SemaphoreType.DMA],
            compiler_params=limit(8),
            name="tables",
        )(mode_x, mode_y, mode_z, source_fine, source_coarse, par)
        of_fine, of_coarse = made[:4], made[4:]

        side_a = lax.ppermute(side_a, axes, beside(bits[0], True))
        side_b = lax.ppermute(side_b, axes, beside(bits[1], False))
        more = [lax.ppermute(par, "member", [(i, i ^ (2 * d)) for i in range(members)])
                for d in others]
        par = jnp.concatenate([par, side_a[rows:, :LANES], side_b[rows:]] + more, axis=0)
        twin = lax.ppermute(par, "member", [(i, i ^ 1) for i in range(members)])

        groups = tiles * n_coarse * cz // LANES
        part = jax.ShapeDtypeStruct((cx, cz, cy), jnp.float32)
        near, force = pl.pallas_call(
            functools.partial(coarse_near_kernel, tiles, groups, coarse_sizes, n_fine, n_coarse,
                              (height, EDGE * 2, rows // cz)),
            out_shape=(part, level_shapes(cx, cy)[3]),
            in_specs=[VMEM] * 7,
            out_specs=(VMEM, VMEM),
            scratch_shapes=scratch(groups, cx, cy, cx),
            compiler_params=limit(16),
            name="coarse_near",
        )(*of_coarse, par, side_a, side_b)

        fine_groups = tiles * n_fine * nz // LANES
        fine = pl.pallas_call(
            functools.partial(fine_kernel, tiles, fine_groups, fine_sizes, strip, n_fine),
            out_shape=jax.ShapeDtypeStruct((nx // 2, nz // 2, ny // 2), jnp.float32),
            in_specs=[VMEM] * 7 + [HBM],
            out_specs=VMEM,
            scratch_shapes=scratch(2 * fine_groups, nx, ny, nx // 2)
            + [pltpu.VMEM((REACH, height, LANES), jnp.float32)],
            compiler_params=limit(24),
            name="fine_smooth",
        )(*of_fine, par, twin, side_a, near)
        arrived = lax.ppermute(fine, axes, everywhere(owner))

        far = pl.pallas_call(
            functools.partial(coarse_kernel, tiles, groups, coarse_sizes, n_fine, n_coarse),
            out_shape=part,
            in_specs=[VMEM] * 6,
            out_specs=VMEM,
            scratch_shapes=scratch(groups, cx, cy, cx),
            compiler_params=limit(16),
            name="coarse_far",
        )(*of_coarse[:3], force, twin, near)
        return arrived + far

    return jax.shard_map(
        body,
        mesh=mesh,
        in_specs=(
            P("member", None), P("member", None), P("member"), P("member"),
            P(), P(), P(), P("tile", None, None), P(None, None, "tile"),
        ),
        out_specs=P("member", None, "tile"),
        check_vma=False,
    )
```

```python
import functools
import math

import jax
import jax.numpy as jnp
from jax import lax
from jax.experimental import pallas as pl
from jax.experimental.pallas import tpu as pltpu
from jax.sharding import PartitionSpec as P

NODES = 9
SWEEPS = 3
CENTRE = 1.125
HALF_WIDTH = 0.875
SPREAD_RATIO = CENTRE / HALF_WIDTH

LANES = 128
HALO = SWEEPS
REACH = SWEEPS - 1
EDGE = 4
PAD = 8
FAR = -2048.0
TERMS = 16
BLOCK = 8


def sweep_factors(sweep_count):
    previous = 1.0 / SPREAD_RATIO
    factors = []
    for _ in range(sweep_count - 1):
        current = 1.0 / (2.0 * SPREAD_RATIO - previous)
        factors.append((current * previous, 2.0 * current / HALF_WIDTH))
        previous = current
    return factors


(A1, B1), (A2, B2) = sweep_factors(SWEEPS)
FIRST = A1 / B1 + CENTRE - 1.0
KEEP0 = (1.0 - B2 * A1 / B1) / (B1 * B2)
KEEP1 = (1.0 + A2 + B2 / B1 - B2) / B2
SHIFT = 0.5 * (FIRST + KEEP1)
REST = KEEP0 + KEEP1 * FIRST - SHIFT * SHIFT
SCALE = 2.0 / CENTRE * B1 * B2 * SHIFT ** 3
EXACT = lax.Precision.HIGHEST
ROWS = (((0,), (0,)), ((), ()))
COLUMNS = (((1,), (1,)), ((), ()))


def iota(shape, dim):
    return lax.broadcasted_iota(jnp.int32, shape, dim)


def pieces(value):
    high = value.astype(jnp.bfloat16)
    rest = value - high.astype(jnp.float32)
    mid = rest.astype(jnp.bfloat16)
    low = (rest - mid.astype(jnp.float32)).astype(jnp.bfloat16)
    return high, mid, low


def aligned(at):
    return at if isinstance(at, int) else pl.multiple_of(at, 8)


def quarter(b, t, tiles):
    return b ^ t ^ jnp.where(t < tiles // 2, tiles - 1, 0)


class Place:
    def __init__(self, tiles):
        m, t = lax.axis_index("member"), lax.axis_index("tile")
        self.tiles, self.m, self.t = tiles, m, t
        self.a, self.b = m % 2, m // 2
        self.half = self.a ^ (t % 2)

    def beside(self, outward):
        step = jnp.where(self.half == 1, 1, -1)
        to = self.t + (step if outward else -step)
        return jnp.where((to >= 0) & (to < self.tiles), to, self.t)


def prep_kernel(tiles, nx, ny, cx, bits, nf_hbm, nc_hbm, wf_ref, wc_ref, sf_ref, sc_hbm,
                a_ref, b_ref, par_ref, plane_ref, nf_ref, nc_ref, sc_ref, sems):
    here = Place(tiles)
    strip, nz, full_y = sf_ref.shape
    full_x, cz, cy = sc_hbm.shape
    height = ny + 2 * EDGE
    start = jnp.where(here.half == 1, strip - REACH, 0)
    copy = pltpu.make_async_copy(sf_ref.at[pl.ds(start, REACH)], plane_ref, sems.at[0])
    copy.start()
    window = cx + 2 * REACH
    lows = [jnp.clip(cx * ((here.b ^ bit) * 2 + here.a) - REACH, 0, full_x - window) for bit in bits]
    blocks = [pltpu.make_async_copy(sc_hbm.at[pl.ds(lows[k], window)], sc_ref.at[k], sems.at[3 + k])
              for k in range(2)]
    nodes = [pltpu.make_async_copy(nf_hbm, nf_ref, sems.at[1]),
             pltpu.make_async_copy(nc_hbm, nc_ref, sems.at[2])]
    for item in nodes + blocks:
        item.start()
    for item in nodes:
        item.wait()

    def node_values(ref):
        nodes = ref[...]
        out = jnp.zeros(nodes.shape, jnp.float32)
        for k in range(NODES):
            out = jnp.where(nodes == k, math.cos(math.pi * k / (NODES - 1)), out)
        return out

    n_fine, terms = nf_ref.shape
    n_coarse = nc_ref.shape[0]
    row, lane = iota((BLOCK, LANES), 0), iota((BLOCK, LANES), 1)
    base = jnp.where((lane == terms) | (lane == terms + 1), 1.0, 0.0)
    for k in range(n_fine + n_coarse):
        weight = wf_ref[k] if k < n_fine else wc_ref[k - n_fine]
        base = jnp.where((row == k) & (lane == terms + 2), weight.astype(jnp.float32), base)
    par_ref[...] = base
    par_ref[0:n_fine, 0:terms] = node_values(nf_ref)
    par_ref[n_fine:n_fine + n_coarse, 0:terms] = node_values(nc_ref)

    rows = REACH * nz
    per_group = rows // cz
    spot = iota((rows, LANES), 1)

    for item in blocks:
        item.wait()

    def coarse_side(side, last, at):
        shifted = cx * ((here.b ^ bits[side]) * 2 + here.a) - REACH - lows[side]
        total = jnp.zeros((rows, LANES), jnp.float32)
        for group in range((cx + 2 * REACH) // per_group):
            parts = [sc_ref[side, jnp.clip(shifted + group * per_group + k, 0, window - 1)]
                     for k in range(per_group)]
            block = jnp.concatenate(parts, axis=0)
            block = jnp.concatenate([block] * (LANES // cy), axis=1)
            to = at + REACH * group
            shift = jnp.where(last, (to - cy + REACH) % LANES, to % LANES)
            block = pltpu.roll(block, shift, 1)
            total = jnp.where((spot >= to) & (spot < to + REACH), block, total)
        return total

    b_ref[0:rows, :] = coarse_side(1, here.half == 0, EDGE * 2)
    edge = coarse_side(0, here.half == 1, height % LANES)
    b_ref[rows:rows + BLOCK, :] = par_ref[...]
    a_ref[rows:rows + BLOCK, 0:LANES] = par_ref[...]

    target = quarter(here.b ^ bits[0], here.beside(True), tiles)
    shift = (EDGE + full_y - ny * target) % full_y
    copy.wait()
    for k in range(REACH):
        turned = pltpu.roll(plane_ref[k], shift, 1)
        part = slice(k * nz, (k + 1) * nz)
        for col in range(a_ref.shape[1] // LANES):
            block = turned[:, col * LANES:(col + 1) * LANES]
            if col == height // LANES:
                block = jnp.where(iota((nz, LANES), 1) < height % LANES, block, edge[part])
            a_ref[part, col * LANES:(col + 1) * LANES] = block


def factors(ratio, terms, nx, ny, nz, x0, y0, full_x, full_y, tx_ref, ty_ref,
            xb_ref, yt_ref, zt_ref):
    nxe, height = nx + 2 * HALO, ny + 2 * EDGE
    row = iota((TERMS, LANES), 0)
    xw = pltpu.roll(tx_ref[0], (ratio * (HALO - x0) + 2 * LANES) % LANES, 1)
    if ratio == 2:
        xw = 0.5 * (xw + pltpu.roll(xw, LANES - 1, 1))
    for i in range(nxe):
        at = x0 - HALO + i
        far = jnp.where((at < 0) | (at >= full_x), FAR, 0.0)
        col = jnp.broadcast_to(xw[:, ratio * i:ratio * i + 1], (TERMS, LANES))
        xb_ref[i] = jnp.where(row == terms, 1.0, jnp.where(row == terms + 1, far, col))
    span = -(-ratio * height // LANES) * LANES
    yw = pltpu.roll(ty_ref[...], (ratio * (EDGE - y0) + ratio * full_y) % (ratio * full_y), 1)
    yw = jnp.concatenate([yw[:, :span]] * 6, axis=0)
    pick = jnp.where(iota((height, span), 1) // ratio == iota((height, span), 0), 1.0 / ratio, 0.0)
    yt = lax.dot_general(pick, yw, COLUMNS, precision=EXACT, preferred_element_type=jnp.float32)
    lane = iota(yt.shape, 1)
    at = y0 - EDGE + iota(yt.shape, 0)
    far = jnp.where((at < 0) | (at >= full_y), FAR, 0.0)
    yt = jnp.where(lane % TERMS == terms, far, jnp.where(lane % TERMS == terms + 1, 1.0, yt))
    high, mid, low = (part.astype(jnp.float32) for part in pieces(yt))
    yt_ref[...] = jnp.where(lane < 3 * TERMS, high, jnp.where(lane < 5 * TERMS, mid, low)).astype(
        jnp.bfloat16)
    down, across = iota((LANES, LANES), 0), iota((LANES, LANES), 1)
    pick = jnp.where(down // ratio == across % nz, 1.0 / ratio, 0.0)
    zt = jnp.dot(tx_ref[1], pick, precision=EXACT, preferred_element_type=jnp.float32)
    zt_ref[...] = jnp.where((row == terms) | (row == terms + 1), 1.0, zt)


def members_of(pars, groups, nz, first_row, per_device, zt_ref, yz_ref):
    weights = []
    for par_ref in pars:
        size = par_ref.shape[0]
        for g in range(groups):
            member = (LANES // nz) * g + iota((size, LANES), 1) // nz
            source = BLOCK * (member // per_device) + first_row + member % per_device
            pick = jnp.where(iota((size, LANES), 0) == source, 1.0, 0.0)
            named = lax.dot_general(par_ref[:, 0:TERMS], pick, ROWS, precision=EXACT,
                                    preferred_element_type=jnp.float32)
            yz_ref[len(weights)] = named * zt_ref[...]
            weights.append(named[TERMS - 2:TERMS - 1, :])
    return weights


def chunks(count, run):
    for k in range(count):
        run(k)


def sweeps(groups, nx, ny, nz, x0, y0, full_x, full_y, pair, weights,
           xb_ref, yt_ref, yz_ref, force, c_ref, kz_ref, q_ref, d_ref, e_ref, u_ref, finish):
    nxe, height = nx + 2 * HALO, ny + 2 * EDGE

    def conduct(i, carry):
        row = xb_ref[i]
        for g in range(groups):
            high, middle, low = pieces(row * yz_ref[g])
            stacked = jnp.concatenate([high, middle, low, high, middle, high], axis=0)
            power = jnp.dot(yt_ref[...], stacked, preferred_element_type=jnp.float32)
            c_ref[g, i, pl.ds(PAD, height), :] = jnp.exp(power)
        return carry

    lax.fori_loop(0, nxe, conduct, 0, unroll=nxe)

    lane = iota((8, LANES), 1) % nz
    is_last, is_first = lane == nz - 1, lane == 0

    def start(k):
        at = aligned(PAD + 8 * k)
        here, up, down = pl.ds(at, 8), pl.ds(at + 1, 8), pl.ds(at - 1, 8)
        own = pl.ds(aligned(8 * k), 8)
        for g in range(groups):
            before, c0 = c_ref[g, 0, here, :], c_ref[g, 1, here, :]
            for i in range(1, nxe - 1):
                after = c_ref[g, i + 1, here, :]
                zp = jnp.where(is_last, 0.0, pltpu.roll(c0, LANES - 1, 1))
                zm = jnp.where(is_first, 0.0, pltpu.roll(c0, 1, 1))
                total = (6.0 * c0 + (before + after)) + (
                    (c_ref[g, i, up, :] + c_ref[g, i, down, :]) + (zp + zm))
                q = (1.0 / SHIFT) / total
                q_ref[g, i, here, :] = q
                d_ref[g, i, here, :] = force(i - 1, own) * q
                kz_ref[g, i, here, :] = jnp.where(is_last, 0.0, c0 + zp)
                before, c0 = c0, after

    chunks(height // 8, start)

    def clear_planes(planes):
        for g in range(groups):
            for i in planes:
                zero = jnp.zeros((height, LANES), jnp.float32)
                q_ref[g, i, pl.ds(PAD, height), :] = zero
                d_ref[g, i, pl.ds(PAD, height), :] = zero

    def clear_rows(at):
        for g in range(groups):
            for i in range(1, nxe - 1):
                zero = jnp.zeros((EDGE, LANES), jnp.float32)
                q_ref[g, i, pl.ds(PAD + at, EDGE), :] = zero
                d_ref[g, i, pl.ds(PAD + at, EDGE), :] = zero

    pl.when(x0 == 0)(lambda: clear_planes(range(1, HALO)))
    pl.when(x0 + nx == full_x)(lambda: clear_planes(range(nx + HALO, nxe - 1)))
    pl.when(y0 == 0)(lambda: clear_rows(0))
    pl.when(y0 + ny == full_y)(lambda: clear_rows(EDGE + ny))

    def walk(g, v_ref, first, last, here, up, down):
        c0, v0 = c_ref[g, first, here, :], v_ref[g, first, here, :]
        v_before = v_ref[g, first - 1, here, :]
        k_before = c_ref[g, first - 1, here, :] + c0
        for i in range(first, last):
            c_after, v_after = c_ref[g, i + 1, here, :], v_ref[g, i + 1, here, :]
            k_after = c0 + c_after
            kz = kz_ref[g, i, here, :]
            along_x = k_after * v_after + k_before * v_before
            along_y = ((c0 + c_ref[g, i, up, :]) * v_ref[g, i, up, :]
                       + (c0 + c_ref[g, i, down, :]) * v_ref[g, i, down, :])
            along_z = kz * pltpu.roll(v0, LANES - 1, 1) + pltpu.roll(kz * v0, 1, 1)
            yield i, v0 + q_ref[g, i, here, :] * ((along_x + along_y) + along_z)
            c0, v0, v_before, k_before = c_after, v_after, v0, k_after

    def first(k):
        at = aligned(PAD + 8 * k)
        here, up, down = pl.ds(at, 8), pl.ds(at + 1, 8), pl.ds(at - 1, 8)
        for g in range(groups):
            for i, value in walk(g, d_ref, 2, nxe - 2, here, up, down):
                e_ref[g, i, here, :] = value

    chunks(height // 8, first)

    step = 2 if pair else 1
    scale = SCALE * (0.125 if pair else 1.0)
    keep = REST / (SHIFT * SHIFT)

    def second(k):
        at = PAD + EDGE + 8 * k
        here, up, down = pl.ds(at, 8), pl.ds(at + 1, 8), pl.ds(at - 1, 8)
        out = [None] * (nx // step)
        for g in range(groups):
            gain = jnp.broadcast_to(scale * weights[g], (8, LANES))
            held = None
            for i, value in walk(g, e_ref, HALO, nx + HALO, here, up, down):
                value = value + keep * d_ref[g, i, here, :]
                j = i - HALO
                if j % step:
                    value = held + value
                held = value
                if j % step == step - 1:
                    value = gain * value
                    out[j // step] = value if g == 0 else out[j // step] + value
        for j, value in enumerate(out):
            u_ref[j, pl.ds(aligned(8 * k), 8), :] = value

    chunks(ny // 8, second)

    out_z = nz // step
    match = iota((out_z, 3 * LANES), 1) % nz // step == iota((out_z, 3 * LANES), 0)
    gather = jnp.where(match, 1.0, 0.0).astype(jnp.bfloat16)
    for j in range(nx // step):
        if pair:
            total = (u_ref[j, pl.ds(0, ny // 2, stride=2), :]
                     + u_ref[j, pl.ds(1, ny // 2, stride=2), :])
        else:
            total = u_ref[j]
        stacked = jnp.concatenate(pieces(total), axis=1)
        finish(j, lax.dot_general(gather, stacked, COLUMNS, preferred_element_type=jnp.float32))


def spread_of(nz):
    match = iota((3 * nz, LANES), 0) % nz == iota((3 * nz, LANES), 1) % nz
    return jnp.where(match, 1.0, 0.0).astype(jnp.bfloat16)


def force_of(source, spread):
    return lax.dot_general(jnp.concatenate(pieces(source), axis=0), spread, ROWS,
                           preferred_element_type=jnp.float32)


def fine_place(here, strip, nx, ny):
    return here.t * strip + here.half * nx, quarter(here.b, here.t, here.tiles) * ny


def table_kernel(tiles, fine_sizes, coarse_sizes, mx_ref, my_ref, mz_ref, sf_ref, sc_ref, order_ref,
                 fx_ref, fy_ref, fz_ref, ff_ref, cx_ref, cy_ref, cz_ref, cf_ref,
                 tx_ref, ty_ref, own_ref, sem):
    here = Place(tiles)
    nx, ny, nz, full_x, full_y = fine_sizes
    strip = sf_ref.shape[0]
    count = nx + REACH
    copy = pltpu.make_async_copy(
        sf_ref.at[pl.ds(jnp.where(here.half == 0, 0, strip - count), count)], own_ref, sem)
    copy.start()
    terms = mx_ref.shape[0]
    tx_ref[...] = jnp.zeros_like(tx_ref)
    tx_ref[0, 0:terms, 0:mx_ref.shape[1]] = mx_ref[...]
    tx_ref[1, 0:terms, 0:mz_ref.shape[1]] = mz_ref[...]
    ty_ref[...] = jnp.zeros_like(ty_ref)
    ty_ref[0:terms, :] = my_ref[...]
    x0, y0 = fine_place(here, strip, nx, ny)
    factors(1, terms, nx, ny, nz, x0, y0, full_x, full_y, tx_ref, ty_ref, fx_ref, fy_ref, fz_ref)
    shift = (EDGE + full_y - y0) % full_y

    nx, ny, nz, full_x, full_y = coarse_sizes
    x0 = here.m * nx
    factors(2, terms, nx, ny, nz, x0, here.t * ny, full_x, full_y, tx_ref, ty_ref,
            cx_ref, cy_ref, cz_ref)
    spread = spread_of(nz)
    for k in range(nx + 2 * REACH):
        x = jnp.clip(x0 - REACH + k, 0, full_x - 1)
        cf_ref[k] = jnp.zeros_like(cf_ref[k])
        cf_ref[k, EDGE:EDGE + ny, :] = force_of(sc_ref[x], spread)

    copy.wait()
    height = ff_ref.shape[1]
    spread = spread_of(fine_sizes[2])

    def place(k):
        source = pltpu.roll(own_ref[k], shift, 1)[:, :height]
        ff_ref[k + REACH * (1 - here.half)] = force_of(source, spread)

    chunks(count, place)


def fine_kernel(tiles, groups, sizes, strip, per_device,
                x_ref, y_ref, z_ref, f_ref, one_ref, two_ref, side_ref, order_ref, out_ref,
                yz_ref, c_ref, kz_ref, q_ref, d_ref, e_ref, u_ref, edge_ref):
    here = Place(tiles)
    nx, ny, nz, full_x, full_y = sizes
    height = ny + 2 * EDGE
    x0, y0 = fine_place(here, strip, nx, ny)
    weights = members_of((one_ref, two_ref), groups, nz, 0, per_device, z_ref, yz_ref)
    spread = spread_of(nz)
    for k in range(REACH):
        edge_ref[k] = force_of(side_ref[k * nz:(k + 1) * nz, :height], spread)
    count = nx + REACH

    def force(k, rows):
        if k < REACH:
            return jnp.where(here.half == 0, edge_ref[k, rows, :], f_ref[k, rows, :])
        if k >= count:
            return jnp.where(here.half == 0, f_ref[k, rows, :], edge_ref[k - count, rows, :])
        return f_ref[k, rows, :]

    def finish(j, value):
        out_ref[j] = value

    sweeps(2 * groups, nx, ny, nz, x0, y0, full_x, full_y, True, weights, x_ref, y_ref, yz_ref,
           force, c_ref, kz_ref, q_ref, d_ref, e_ref, u_ref, finish)


def coarse_kernel(tiles, groups, sizes, first_row, per_device,
                  x_ref, y_ref, z_ref, f_ref, par_ref, base_ref, out_ref,
                  yz_ref, c_ref, kz_ref, q_ref, d_ref, e_ref, u_ref):
    here = Place(tiles)
    nx, ny, nz, full_x, full_y = sizes
    weights = members_of((par_ref,), groups, nz, first_row, per_device, z_ref, yz_ref)

    def force(k, rows):
        return f_ref[k, rows, :]

    def finish(j, value):
        out_ref[j] = value if base_ref is None else base_ref[j] + value

    sweeps(groups, nx, ny, nz, here.m * nx, here.t * ny, full_x, full_y, False, weights, x_ref,
           y_ref, yz_ref, force, c_ref, kz_ref, q_ref, d_ref, e_ref, u_ref, finish)


def coarse_near_kernel(tiles, groups, sizes, first_row, per_device, side_at,
                       x_ref, y_ref, z_ref, f_ref, par_ref, a_ref, b_ref, out_ref, full_ref,
                       *scratch_refs):
    here = Place(tiles)
    nx, ny, nz, _, _ = sizes
    spread = spread_of(nz)
    per_group = side_at[2]
    for k in range(nx + 2 * REACH):
        full_ref[k] = f_ref[k]
        rows = slice(k % per_group * nz, (k % per_group + 1) * nz)
        found = []
        for ref, at in ((a_ref, side_at[0]), (b_ref, side_at[1])):
            low = at // 16 * 16
            block = force_of(ref[rows, low:low + 16], spread)
            at = at - low + REACH * (k // per_group)
            found.append(block[at:at + REACH])
        full_ref[k, EDGE - REACH:EDGE, :] = jnp.where(here.half == 0, found[0], found[1])
        full_ref[k, EDGE + ny:EDGE + ny + REACH, :] = jnp.where(
            here.half == 0, found[1], found[0])
    coarse_kernel(tiles, groups, sizes, first_row, per_device, x_ref, y_ref, z_ref, full_ref,
                  par_ref, None, out_ref, *scratch_refs)


def scratch(groups, nx, ny, count):
    nxe, height = nx + 2 * HALO, ny + 2 * EDGE
    grid = pltpu.VMEM((groups, nxe, height + 2 * PAD, LANES), jnp.float32)
    return [pltpu.VMEM((groups, TERMS, LANES), jnp.float32), grid, grid, grid, grid, grid,
            pltpu.VMEM((count, ny, LANES), jnp.float32)]


def level_shapes(nx, ny):
    nxe, height = nx + 2 * HALO, ny + 2 * EDGE
    return (jax.ShapeDtypeStruct((nxe, TERMS, LANES), jnp.float32),
            jax.ShapeDtypeStruct((height, 6 * TERMS), jnp.bfloat16),
            jax.ShapeDtypeStruct((TERMS, LANES), jnp.float32),
            jax.ShapeDtypeStruct((nx + 2 * REACH, height, LANES), jnp.float32))


def limit(mebibytes):
    return pltpu.CompilerParams(vmem_limit_bytes=mebibytes << 20)


VMEM = pl.BlockSpec(memory_space=pltpu.VMEM)
SMEM = pl.BlockSpec(memory_space=pltpu.SMEM)
HBM = pl.BlockSpec(memory_space=pl.ANY)
FIXED = pl.BlockSpec(memory_space=pltpu.HBM)


def solution(mesh):
    members, tiles = mesh.shape["member"], mesh.shape["tile"]
    assert members == 2 * tiles and tiles >= 4
    axes = ("member", "tile")
    bits = (tiles // 2, tiles // 4)
    others = [d for d in range(1, tiles) if d not in bits]

    def flat(b, a, t):
        return (b * 2 + a) * tiles + t

    def everywhere(rule):
        return [(flat(b, a, t), flat(*rule(b, a, t)))
                for b in range(tiles) for a in range(2) for t in range(tiles)]

    def beside(bit, outward):
        def rule(b, a, t):
            step = 1 if a ^ (t % 2) else -1
            to = t + (step if outward else -step)
            return b ^ bit, a, to if 0 <= to < tiles else t
        return everywhere(rule)

    def owner(b, a, t):
        return t, a ^ (t % 2), b ^ t ^ (tiles - 1 if t < tiles // 2 else 0)

    def body(node_fine, node_coarse, weight_fine, weight_coarse, mode_x, mode_y, mode_z,
             source_fine, source_coarse):
        strip, nz, full_y = source_fine.shape
        full_cx, cz, cy = source_coarse.shape
        full_x = mode_x.shape[1]
        nx, ny, cx = full_x // members, full_y // tiles, full_cx // members
        n_fine, n_coarse = node_fine.shape[0], node_coarse.shape[0]
        height = ny + 2 * EDGE
        rows = REACH * nz
        width = -(-(height + REACH * 2) // LANES) * LANES
        fine_sizes = nx, ny, nz, full_x, full_y
        coarse_sizes = cx, cy, cz, full_cx, cy * tiles

        side_a, side_b, par = pl.pallas_call(
            functools.partial(prep_kernel, tiles, nx, ny, cx, bits),
            out_shape=(jax.ShapeDtypeStruct((rows + BLOCK, width), jnp.float32),
                       jax.ShapeDtypeStruct((rows + BLOCK, LANES), jnp.float32),
                       jax.ShapeDtypeStruct((BLOCK, LANES), jnp.float32)),
            in_specs=[FIXED, FIXED, SMEM, SMEM, FIXED, FIXED],
            out_specs=(VMEM, VMEM, VMEM),
            scratch_shapes=[pltpu.VMEM((REACH, nz, full_y), jnp.float32),
                            pltpu.VMEM(node_fine.shape, jnp.int32),
                            pltpu.VMEM(node_coarse.shape, jnp.int32),
                            pltpu.VMEM((2, cx + 2 * REACH, cz, cy), jnp.float32),
                            pltpu.SemaphoreType.DMA((5,))],
            compiler_params=pltpu.CompilerParams(vmem_limit_bytes=67043328 - (200 << 10)),
            name="prep",
        )(node_fine, node_coarse, weight_fine, weight_coarse, source_fine, source_coarse)

        made = pl.pallas_call(
            functools.partial(table_kernel, tiles, fine_sizes, coarse_sizes),
            out_shape=level_shapes(nx, ny) + level_shapes(cx, cy),
            in_specs=[VMEM] * 3 + [HBM, VMEM, HBM],
            out_specs=(VMEM,) * 8,
            scratch_shapes=[pltpu.VMEM((2, TERMS, LANES), jnp.float32),
                            pltpu.VMEM((TERMS, full_y), jnp.float32),
                            pltpu.VMEM((nx + REACH, nz, full_y), jnp.float32),
                            pltpu.SemaphoreType.DMA],
            compiler_params=limit(8),
            name="tables",
        )(mode_x, mode_y, mode_z, source_fine, source_coarse, par)

        side_a = lax.ppermute(side_a, axes, beside(bits[0], True))
        side_b = lax.ppermute(side_b, axes, beside(bits[1], False))
        more = [lax.ppermute(par, "member", [(i, i ^ (2 * d)) for i in range(members)])
                for d in others]
        par, made = lax.optimization_barrier((par, made))
        of_fine, of_coarse = made[:4], made[4:]
        par = jnp.concatenate([par, side_a[rows:, :LANES], side_b[rows:]] + more, axis=0)
        twin = lax.ppermute(par, "member", [(i, i ^ 1) for i in range(members)])

        groups = tiles * n_coarse * cz // LANES
        part = jax.ShapeDtypeStruct((cx, cz, cy), jnp.float32)
        near, force = pl.pallas_call(
            functools.partial(coarse_near_kernel, tiles, groups, coarse_sizes, n_fine, n_coarse,
                              (height, EDGE * 2, rows // cz)),
            out_shape=(part, level_shapes(cx, cy)[3]),
            in_specs=[VMEM] * 7,
            out_specs=(VMEM, VMEM),
            scratch_shapes=scratch(groups, cx, cy, cx),
            compiler_params=limit(16),
            name="coarse_near",
        )(*of_coarse, par, side_a, side_b)

        fine_groups = tiles * n_fine * nz // LANES
        fine = pl.pallas_call(
            functools.partial(fine_kernel, tiles, fine_groups, fine_sizes, strip, n_fine),
            out_shape=jax.ShapeDtypeStruct((nx // 2, nz // 2, ny // 2), jnp.float32),
            in_specs=[VMEM] * 7 + [HBM],
            out_specs=VMEM,
            scratch_shapes=scratch(2 * fine_groups, nx, ny, nx // 2)
            + [pltpu.VMEM((REACH, height, LANES), jnp.float32)],
            compiler_params=limit(24),
            name="fine_smooth",
        )(*of_fine, par, twin, side_a, near)
        arrived = lax.ppermute(fine, axes, everywhere(owner))

        far = pl.pallas_call(
            functools.partial(coarse_kernel, tiles, groups, coarse_sizes, n_fine, n_coarse),
            out_shape=part,
            in_specs=[VMEM] * 6,
            out_specs=VMEM,
            scratch_shapes=scratch(groups, cx, cy, cx),
            compiler_params=limit(16),
            name="coarse_far",
        )(*of_coarse[:3], force, twin, near)
        return arrived + far

    return jax.shard_map(
        body,
        mesh=mesh,
        in_specs=(
            P("member", None), P("member", None), P("member"), P("member"),
            P(), P(), P(), P("tile", None, None), P(None, None, "tile"),
        ),
        out_specs=P("member", None, "tile"),
        check_vma=False,
    )
```

```python
import functools
import math

import jax
import jax.numpy as jnp
from jax import lax
from jax.experimental import pallas as pl
from jax.experimental.pallas import tpu as pltpu
from jax.sharding import PartitionSpec as P

NODES = 9
SWEEPS = 3
CENTRE = 1.125
HALF_WIDTH = 0.875
SPREAD_RATIO = CENTRE / HALF_WIDTH

LANES = 128
HALO = SWEEPS
REACH = SWEEPS - 1
EDGE = 4
PAD = 8
FAR = -2048.0
TERMS = 16
BLOCK = 8


def sweep_factors(sweep_count):
    previous = 1.0 / SPREAD_RATIO
    factors = []
    for _ in range(sweep_count - 1):
        current = 1.0 / (2.0 * SPREAD_RATIO - previous)
        factors.append((current * previous, 2.0 * current / HALF_WIDTH))
        previous = current
    return factors


(A1, B1), (A2, B2) = sweep_factors(SWEEPS)
FIRST = A1 / B1 + CENTRE - 1.0
KEEP0 = (1.0 - B2 * A1 / B1) / (B1 * B2)
KEEP1 = (1.0 + A2 + B2 / B1 - B2) / B2
SHIFT = 0.5 * (FIRST + KEEP1)
REST = KEEP0 + KEEP1 * FIRST - SHIFT * SHIFT
SCALE = 2.0 / CENTRE * B1 * B2 * SHIFT ** 3
EXACT = lax.Precision.HIGHEST
ROWS = (((0,), (0,)), ((), ()))
COLUMNS = (((1,), (1,)), ((), ()))


def iota(shape, dim):
    return lax.broadcasted_iota(jnp.int32, shape, dim)


def pieces(value):
    high = value.astype(jnp.bfloat16)
    rest = value - high.astype(jnp.float32)
    mid = rest.astype(jnp.bfloat16)
    low = (rest - mid.astype(jnp.float32)).astype(jnp.bfloat16)
    return high, mid, low


def aligned(at):
    return at if isinstance(at, int) else pl.multiple_of(at, 8)


def quarter(b, t, tiles):
    return b ^ t ^ jnp.where(t < tiles // 2, tiles - 1, 0)


class Place:
    def __init__(self, tiles):
        m, t = lax.axis_index("member"), lax.axis_index("tile")
        self.tiles, self.m, self.t = tiles, m, t
        self.a, self.b = m % 2, m // 2
        self.half = self.a ^ (t % 2)

    def beside(self, outward):
        step = jnp.where(self.half == 1, 1, -1)
        to = self.t + (step if outward else -step)
        return jnp.where((to >= 0) & (to < self.tiles), to, self.t)


def prep_kernel(tiles, nx, ny, cx, bits, nf_hbm, nc_hbm, wf_ref, wc_ref, sf_ref, sc_hbm,
                a_ref, b_ref, par_ref, plane_ref, nf_ref, nc_ref, sc_ref, sems):
    here = Place(tiles)
    strip, nz, full_y = sf_ref.shape
    full_x, cz, cy = sc_hbm.shape
    height = ny + 2 * EDGE
    start = jnp.where(here.half == 1, strip - REACH, 0)
    copy = pltpu.make_async_copy(sf_ref.at[pl.ds(start, REACH)], plane_ref, sems.at[0])
    copy.start()
    window = cx + 2 * REACH
    lows = [jnp.clip(cx * ((here.b ^ bit) * 2 + here.a) - REACH, 0, full_x - window) for bit in bits]
    blocks = [pltpu.make_async_copy(sc_hbm.at[pl.ds(lows[k], window)], sc_ref.at[k], sems.at[3 + k])
              for k in range(2)]
    nodes = [pltpu.make_async_copy(nf_hbm, nf_ref, sems.at[1]),
             pltpu.make_async_copy(nc_hbm, nc_ref, sems.at[2])]
    for item in nodes + blocks:
        item.start()
    for item in nodes:
        item.wait()

    def node_values(ref):
        nodes = ref[...]
        out = jnp.zeros(nodes.shape, jnp.float32)
        for k in range(NODES):
            out = jnp.where(nodes == k, math.cos(math.pi * k / (NODES - 1)), out)
        return out

    n_fine, terms = nf_ref.shape
    n_coarse = nc_ref.shape[0]
    row, lane = iota((BLOCK, LANES), 0), iota((BLOCK, LANES), 1)
    base = jnp.where((lane == terms) | (lane == terms + 1), 1.0, 0.0)
    for k in range(n_fine + n_coarse):
        weight = wf_ref[k] if k < n_fine else wc_ref[k - n_fine]
        base = jnp.where((row == k) & (lane == terms + 2), weight.astype(jnp.float32), base)
    par_ref[...] = base
    par_ref[0:n_fine, 0:terms] = node_values(nf_ref)
    par_ref[n_fine:n_fine + n_coarse, 0:terms] = node_values(nc_ref)

    rows = REACH * nz
    per_group = rows // cz
    spot = iota((rows, LANES), 1)

    for item in blocks:
        item.wait()

    def coarse_side(side, last, at):
        shifted = cx * ((here.b ^ bits[side]) * 2 + here.a) - REACH - lows[side]
        total = jnp.zeros((rows, LANES), jnp.float32)
        for group in range((cx + 2 * REACH) // per_group):
            parts = [sc_ref[side, jnp.clip(shifted + group * per_group + k, 0, window - 1)]
                     for k in range(per_group)]
            block = jnp.concatenate(parts, axis=0)
            block = jnp.concatenate([block] * (LANES // cy), axis=1)
            to = at + REACH * group
            shift = jnp.where(last, (to - cy + REACH) % LANES, to % LANES)
            block = pltpu.roll(block, shift, 1)
            total = jnp.where((spot >= to) & (spot < to + REACH), block, total)
        return total

    b_ref[0:rows, :] = coarse_side(1, here.half == 0, EDGE * 2)
    edge = coarse_side(0, here.half == 1, height % LANES)
    b_ref[rows:rows + BLOCK, :] = par_ref[...]
    a_ref[rows:rows + BLOCK, 0:LANES] = par_ref[...]

    target = quarter(here.b ^ bits[0], here.beside(True), tiles)
    shift = (EDGE + full_y - ny * target) % full_y
    copy.wait()
    for k in range(REACH):
        turned = pltpu.roll(plane_ref[k], shift, 1)
        part = slice(k * nz, (k + 1) * nz)
        for col in range(a_ref.shape[1] // LANES):
            block = turned[:, col * LANES:(col + 1) * LANES]
            if col == height // LANES:
                block = jnp.where(iota((nz, LANES), 1) < height % LANES, block, edge[part])
            a_ref[part, col * LANES:(col + 1) * LANES] = block


def factors(ratio, terms, nx, ny, nz, x0, y0, full_x, full_y, tx_ref, ty_ref,
            xb_ref, yt_ref, zt_ref):
    nxe, height = nx + 2 * HALO, ny + 2 * EDGE
    row = iota((TERMS, LANES), 0)
    xw = pltpu.roll(tx_ref[0], (ratio * (HALO - x0) + 2 * LANES) % LANES, 1)
    if ratio == 2:
        xw = 0.5 * (xw + pltpu.roll(xw, LANES - 1, 1))
    for i in range(nxe):
        at = x0 - HALO + i
        far = jnp.where((at < 0) | (at >= full_x), FAR, 0.0)
        col = jnp.broadcast_to(xw[:, ratio * i:ratio * i + 1], (TERMS, LANES))
        xb_ref[i] = jnp.where(row == terms, 1.0, jnp.where(row == terms + 1, far, col))
    span = -(-ratio * height // LANES) * LANES
    yw = pltpu.roll(ty_ref[...], (ratio * (EDGE - y0) + ratio * full_y) % (ratio * full_y), 1)
    yw = jnp.concatenate([yw[:, :span]] * 6, axis=0)
    pick = jnp.where(iota((height, span), 1) // ratio == iota((height, span), 0), 1.0 / ratio, 0.0)
    yt = lax.dot_general(pick, yw, COLUMNS, precision=EXACT, preferred_element_type=jnp.float32)
    lane = iota(yt.shape, 1)
    at = y0 - EDGE + iota(yt.shape, 0)
    far = jnp.where((at < 0) | (at >= full_y), FAR, 0.0)
    yt = jnp.where(lane % TERMS == terms, far, jnp.where(lane % TERMS == terms + 1, 1.0, yt))
    high, mid, low = (part.astype(jnp.float32) for part in pieces(yt))
    yt_ref[...] = jnp.where(lane < 3 * TERMS, high, jnp.where(lane < 5 * TERMS, mid, low)).astype(
        jnp.bfloat16)
    down, across = iota((LANES, LANES), 0), iota((LANES, LANES), 1)
    pick = jnp.where(down // ratio == across % nz, 1.0 / ratio, 0.0)
    zt = jnp.dot(tx_ref[1], pick, precision=EXACT, preferred_element_type=jnp.float32)
    zt_ref[...] = jnp.where((row == terms) | (row == terms + 1), 1.0, zt)


def members_of(pars, nz, first_row, per_device, zt_ref, yz_ref):
    weights = []
    for par_ref, groups in pars:
        size = par_ref.shape[0]
        for g in groups:
            member = (LANES // nz) * g + iota((size, LANES), 1) // nz
            source = BLOCK * (member // per_device) + first_row + member % per_device
            pick = jnp.where(iota((size, LANES), 0) == source, 1.0, 0.0)
            named = lax.dot_general(par_ref[:, 0:TERMS], pick, ROWS, precision=EXACT,
                                    preferred_element_type=jnp.float32)
            yz_ref[len(weights)] = named * zt_ref[...]
            weights.append(named[TERMS - 2:TERMS - 1, :])
    return weights


def chunks(count, run):
    for k in range(count):
        run(k)


def sweeps(groups, nx, ny, nz, x0, y0, full_x, full_y, pair, weights,
           xb_ref, yt_ref, yz_ref, force, c_ref, kz_ref, q_ref, d_ref, e_ref, u_ref, finish):
    nxe, height = nx + 2 * HALO, ny + 2 * EDGE

    def conduct(i, carry):
        row = xb_ref[i]
        for g in range(groups):
            high, middle, low = pieces(row * yz_ref[g])
            stacked = jnp.concatenate([high, middle, low, high, middle, high], axis=0)
            power = jnp.dot(yt_ref[...], stacked, preferred_element_type=jnp.float32)
            c_ref[g, i, pl.ds(PAD, height), :] = jnp.exp(power)
        return carry

    lax.fori_loop(0, nxe, conduct, 0, unroll=nxe)

    lane = iota((8, LANES), 1) % nz
    is_last, is_first = lane == nz - 1, lane == 0

    def start(k):
        at = aligned(PAD + 8 * k)
        here, up, down = pl.ds(at, 8), pl.ds(at + 1, 8), pl.ds(at - 1, 8)
        own = pl.ds(aligned(8 * k), 8)
        for g in range(groups):
            before, c0 = c_ref[g, 0, here, :], c_ref[g, 1, here, :]
            for i in range(1, nxe - 1):
                after = c_ref[g, i + 1, here, :]
                zp = jnp.where(is_last, 0.0, pltpu.roll(c0, LANES - 1, 1))
                zm = jnp.where(is_first, 0.0, pltpu.roll(c0, 1, 1))
                total = (6.0 * c0 + (before + after)) + (
                    (c_ref[g, i, up, :] + c_ref[g, i, down, :]) + (zp + zm))
                q = (1.0 / SHIFT) / total
                q_ref[g, i, here, :] = q
                d_ref[g, i, here, :] = force(i - 1, own) * q
                kz_ref[g, i, here, :] = jnp.where(is_last, 0.0, c0 + zp)
                before, c0 = c0, after

    chunks(height // 8, start)

    def clear_planes(planes):
        for g in range(groups):
            for i in planes:
                zero = jnp.zeros((height, LANES), jnp.float32)
                q_ref[g, i, pl.ds(PAD, height), :] = zero
                d_ref[g, i, pl.ds(PAD, height), :] = zero

    def clear_rows(at):
        for g in range(groups):
            for i in range(1, nxe - 1):
                zero = jnp.zeros((EDGE, LANES), jnp.float32)
                q_ref[g, i, pl.ds(PAD + at, EDGE), :] = zero
                d_ref[g, i, pl.ds(PAD + at, EDGE), :] = zero

    pl.when(x0 == 0)(lambda: clear_planes(range(1, HALO)))
    pl.when(x0 + nx == full_x)(lambda: clear_planes(range(nx + HALO, nxe - 1)))
    pl.when(y0 == 0)(lambda: clear_rows(0))
    pl.when(y0 + ny == full_y)(lambda: clear_rows(EDGE + ny))

    def walk(g, v_ref, first, last, here, up, down):
        c0, v0 = c_ref[g, first, here, :], v_ref[g, first, here, :]
        v_before = v_ref[g, first - 1, here, :]
        k_before = c_ref[g, first - 1, here, :] + c0
        for i in range(first, last):
            c_after, v_after = c_ref[g, i + 1, here, :], v_ref[g, i + 1, here, :]
            k_after = c0 + c_after
            kz = kz_ref[g, i, here, :]
            along_x = k_after * v_after + k_before * v_before
            along_y = ((c0 + c_ref[g, i, up, :]) * v_ref[g, i, up, :]
                       + (c0 + c_ref[g, i, down, :]) * v_ref[g, i, down, :])
            along_z = kz * pltpu.roll(v0, LANES - 1, 1) + pltpu.roll(kz * v0, 1, 1)
            yield i, v0 + q_ref[g, i, here, :] * ((along_x + along_y) + along_z)
            c0, v0, v_before, k_before = c_after, v_after, v0, k_after

    def first(k):
        at = aligned(PAD + 8 * k)
        here, up, down = pl.ds(at, 8), pl.ds(at + 1, 8), pl.ds(at - 1, 8)
        for g in range(groups):
            for i, value in walk(g, d_ref, 2, nxe - 2, here, up, down):
                e_ref[g, i, here, :] = value

    chunks(height // 8, first)

    step = 2 if pair else 1
    scale = SCALE * (0.125 if pair else 1.0)
    keep = REST / (SHIFT * SHIFT)

    def second(k):
        at = PAD + EDGE + 8 * k
        here, up, down = pl.ds(at, 8), pl.ds(at + 1, 8), pl.ds(at - 1, 8)
        out = [None] * (nx // step)
        for g in range(groups):
            gain = jnp.broadcast_to(scale * weights[g], (8, LANES))
            held = None
            for i, value in walk(g, e_ref, HALO, nx + HALO, here, up, down):
                value = value + keep * d_ref[g, i, here, :]
                j = i - HALO
                if j % step:
                    value = held + value
                held = value
                if j % step == step - 1:
                    value = gain * value
                    out[j // step] = value if g == 0 else out[j // step] + value
        for j, value in enumerate(out):
            u_ref[j, pl.ds(aligned(8 * k), 8), :] = value

    chunks(ny // 8, second)

    out_z = nz // step
    match = iota((out_z, 3 * LANES), 1) % nz // step == iota((out_z, 3 * LANES), 0)
    gather = jnp.where(match, 1.0, 0.0).astype(jnp.bfloat16)
    for j in range(nx // step):
        if pair:
            total = (u_ref[j, pl.ds(0, ny // 2, stride=2), :]
                     + u_ref[j, pl.ds(1, ny // 2, stride=2), :])
        else:
            total = u_ref[j]
        stacked = jnp.concatenate(pieces(total), axis=1)
        finish(j, lax.dot_general(gather, stacked, COLUMNS, preferred_element_type=jnp.float32))


def spread_of(nz):
    match = iota((3 * nz, LANES), 0) % nz == iota((3 * nz, LANES), 1) % nz
    return jnp.where(match, 1.0, 0.0).astype(jnp.bfloat16)


def force_of(source, spread):
    return lax.dot_general(jnp.concatenate(pieces(source), axis=0), spread, ROWS,
                           preferred_element_type=jnp.float32)


def fine_place(here, strip, nx, ny):
    return here.t * strip + here.half * nx, quarter(here.b, here.t, here.tiles) * ny


def table_kernel(tiles, fine_sizes, coarse_sizes, mx_ref, my_ref, mz_ref, sf_ref, order_ref,
                 fx_ref, fy_ref, fz_ref, ff_ref, cx_ref, cy_ref, cz_ref, tx_ref, ty_ref):
    here = Place(tiles)
    nx, ny, nz, full_x, full_y = fine_sizes
    strip = sf_ref.shape[0]
    count = nx + REACH
    terms = mx_ref.shape[0]
    tx_ref[...] = jnp.zeros_like(tx_ref)
    tx_ref[0, 0:terms, 0:mx_ref.shape[1]] = mx_ref[...]
    tx_ref[1, 0:terms, 0:mz_ref.shape[1]] = mz_ref[...]
    ty_ref[...] = jnp.zeros_like(ty_ref)
    ty_ref[0:terms, :] = my_ref[...]
    x0, y0 = fine_place(here, strip, nx, ny)
    factors(1, terms, nx, ny, nz, x0, y0, full_x, full_y, tx_ref, ty_ref, fx_ref, fy_ref, fz_ref)
    shift = (EDGE + full_y - y0) % full_y
    height = ff_ref.shape[1]
    spread = spread_of(nz)
    low = jnp.where(here.half == 0, 0, strip - count)
    for k in range(count):
        source = pltpu.roll(sf_ref[low + k], shift, 1)[:, :height]
        ff_ref[k + REACH * (1 - here.half)] = force_of(source, spread)

    nx, ny, nz, full_x, full_y = coarse_sizes
    factors(2, terms, nx, ny, nz, here.m * nx, here.t * ny, full_x, full_y, tx_ref, ty_ref,
            cx_ref, cy_ref, cz_ref)


def fine_kernel(tiles, groups, sizes, strip, per_device,
                x_ref, y_ref, z_ref, f_ref, one_ref, two_ref, side_ref, order_ref, out_ref,
                yz_ref, c_ref, kz_ref, q_ref, d_ref, e_ref, u_ref, edge_ref):
    here = Place(tiles)
    nx, ny, nz, full_x, full_y = sizes
    height = ny + 2 * EDGE
    x0, y0 = fine_place(here, strip, nx, ny)
    weights = members_of(((one_ref, range(groups)), (two_ref, range(groups))), nz, 0, per_device, z_ref, yz_ref)
    spread = spread_of(nz)
    for k in range(REACH):
        edge_ref[k] = force_of(side_ref[k * nz:(k + 1) * nz, :height], spread)
    count = nx + REACH

    def force(k, rows):
        if k < REACH:
            return jnp.where(here.half == 0, edge_ref[k, rows, :], f_ref[k, rows, :])
        if k >= count:
            return jnp.where(here.half == 0, f_ref[k, rows, :], edge_ref[k - count, rows, :])
        return f_ref[k, rows, :]

    def finish(j, value):
        out_ref[j] = value

    sweeps(2 * groups, nx, ny, nz, x0, y0, full_x, full_y, True, weights, x_ref, y_ref, yz_ref,
           force, c_ref, kz_ref, q_ref, d_ref, e_ref, u_ref, finish)


def coarse_sweeps(here, sizes, weights, x_ref, y_ref, f_ref, base_ref, out_ref,
                  yz_ref, c_ref, kz_ref, q_ref, d_ref, e_ref, u_ref):
    nx, ny, nz, full_x, full_y = sizes

    def finish(j, value):
        out_ref[j] = value if base_ref is None else base_ref[j] + value

    sweeps(len(weights), nx, ny, nz, here.m * nx, here.t * ny, full_x, full_y, False, weights,
           x_ref, y_ref, yz_ref, lambda k, rows: f_ref[k, rows, :], c_ref, kz_ref, q_ref, d_ref,
           e_ref, u_ref, finish)


def coarse_near_kernel(tiles, groups, sizes, first_row, per_device, side_at,
                       x_ref, y_ref, z_ref, sc_ref, par_ref, a_ref, b_ref, out_ref, full_ref,
                       yz_ref, *grids):
    here = Place(tiles)
    nx, ny, nz, full_x, _ = sizes
    spread = spread_of(nz)
    per_group = side_at[2]
    for k in range(nx + 2 * REACH):
        full_ref[k, 0:8, :] = jnp.zeros((8, LANES), jnp.float32)
        full_ref[k, ny:ny + 2 * EDGE, :] = jnp.zeros((8, LANES), jnp.float32)
        x = jnp.clip(here.m * nx - REACH + k, 0, full_x - 1)
        full_ref[k, EDGE:EDGE + ny, :] = force_of(sc_ref[x], spread)
        rows = slice(k % per_group * nz, (k % per_group + 1) * nz)
        found = []
        for ref, at in ((a_ref, side_at[0]), (b_ref, side_at[1])):
            low = at // 16 * 16
            block = force_of(ref[rows, low:low + 16], spread)
            at = at - low + REACH * (k // per_group)
            found.append(block[at:at + REACH])
        full_ref[k, EDGE - REACH:EDGE, :] = jnp.where(here.half == 0, found[0], found[1])
        full_ref[k, EDGE + ny:EDGE + ny + REACH, :] = jnp.where(
            here.half == 0, found[1], found[0])
    weights = members_of(((par_ref, groups),), nz, first_row, per_device, z_ref, yz_ref)
    coarse_sweeps(here, sizes, weights, x_ref, y_ref, full_ref, None, out_ref, yz_ref, *grids)


def coarse_far_kernel(tiles, groups, twin_groups, sizes, first_row, per_device,
                      x_ref, y_ref, z_ref, f_ref, par_ref, twin_ref, base_ref, out_ref,
                      yz_ref, *grids):
    here = Place(tiles)
    weights = members_of(((par_ref, groups), (twin_ref, twin_groups)), sizes[2], first_row,
                         per_device, z_ref, yz_ref)
    coarse_sweeps(here, sizes, weights, x_ref, y_ref, f_ref, base_ref, out_ref, yz_ref, *grids)


def scratch(groups, nx, ny, count):
    nxe, height = nx + 2 * HALO, ny + 2 * EDGE
    grid = pltpu.VMEM((groups, nxe, height + 2 * PAD, LANES), jnp.float32)
    return [pltpu.VMEM((groups, TERMS, LANES), jnp.float32), grid, grid, grid, grid, grid,
            pltpu.VMEM((count, ny, LANES), jnp.float32)]


def level_shapes(nx, ny):
    nxe, height = nx + 2 * HALO, ny + 2 * EDGE
    return (jax.ShapeDtypeStruct((nxe, TERMS, LANES), jnp.float32),
            jax.ShapeDtypeStruct((height, 6 * TERMS), jnp.bfloat16),
            jax.ShapeDtypeStruct((TERMS, LANES), jnp.float32),
            jax.ShapeDtypeStruct((nx + 2 * REACH, height, LANES), jnp.float32))


def limit(mebibytes):
    return pltpu.CompilerParams(vmem_limit_bytes=mebibytes << 20)


VMEM = pl.BlockSpec(memory_space=pltpu.VMEM)
SMEM = pl.BlockSpec(memory_space=pltpu.SMEM)
HBM = pl.BlockSpec(memory_space=pl.ANY)
FIXED = pl.BlockSpec(memory_space=pltpu.HBM)


def solution(mesh):
    members, tiles = mesh.shape["member"], mesh.shape["tile"]
    assert members == 2 * tiles and tiles >= 4
    axes = ("member", "tile")
    bits = (tiles // 2, tiles // 4)
    others = [d for d in range(1, tiles) if d not in bits]

    def flat(b, a, t):
        return (b * 2 + a) * tiles + t

    def everywhere(rule):
        return [(flat(b, a, t), flat(*rule(b, a, t)))
                for b in range(tiles) for a in range(2) for t in range(tiles)]

    def beside(bit, outward):
        def rule(b, a, t):
            step = 1 if a ^ (t % 2) else -1
            to = t + (step if outward else -step)
            return b ^ bit, a, to if 0 <= to < tiles else t
        return everywhere(rule)

    def owner(b, a, t):
        return t, a ^ (t % 2), b ^ t ^ (tiles - 1 if t < tiles // 2 else 0)

    def body(node_fine, node_coarse, weight_fine, weight_coarse, mode_x, mode_y, mode_z,
             source_fine, source_coarse):
        strip, nz, full_y = source_fine.shape
        full_cx, cz, cy = source_coarse.shape
        full_x = mode_x.shape[1]
        nx, ny, cx = full_x // members, full_y // tiles, full_cx // members
        n_fine, n_coarse = node_fine.shape[0], node_coarse.shape[0]
        height = ny + 2 * EDGE
        rows = REACH * nz
        width = -(-(height + REACH * 2) // LANES) * LANES
        fine_sizes = nx, ny, nz, full_x, full_y
        coarse_sizes = cx, cy, cz, full_cx, cy * tiles

        side_a, side_b, par = pl.pallas_call(
            functools.partial(prep_kernel, tiles, nx, ny, cx, bits),
            out_shape=(jax.ShapeDtypeStruct((rows + BLOCK, width), jnp.float32),
                       jax.ShapeDtypeStruct((rows + BLOCK, LANES), jnp.float32),
                       jax.ShapeDtypeStruct((BLOCK, LANES), jnp.float32)),
            in_specs=[FIXED, FIXED, SMEM, SMEM, FIXED, FIXED],
            out_specs=(VMEM, VMEM, VMEM),
            scratch_shapes=[pltpu.VMEM((REACH, nz, full_y), jnp.float32),
                            pltpu.VMEM(node_fine.shape, jnp.int32),
                            pltpu.VMEM(node_coarse.shape, jnp.int32),
                            pltpu.VMEM((2, cx + 2 * REACH, cz, cy), jnp.float32),
                            pltpu.SemaphoreType.DMA((5,))],
            compiler_params=pltpu.CompilerParams(vmem_limit_bytes=67043328 - (200 << 10)),
            name="prep",
        )(node_fine, node_coarse, weight_fine, weight_coarse, source_fine, source_coarse)

        made = pl.pallas_call(
            functools.partial(table_kernel, tiles, fine_sizes, coarse_sizes),
            out_shape=level_shapes(nx, ny) + level_shapes(cx, cy)[:3],
            in_specs=[VMEM] * 4 + [HBM],
            out_specs=(VMEM,) * 7,
            scratch_shapes=[pltpu.VMEM((2, TERMS, LANES), jnp.float32),
                            pltpu.VMEM((TERMS, full_y), jnp.float32)],
            compiler_params=limit(8),
            name="tables",
        )(mode_x, mode_y, mode_z, source_fine, par)

        side_a = lax.ppermute(side_a, axes, beside(bits[0], True))
        side_b = lax.ppermute(side_b, axes, beside(bits[1], False))
        more = [lax.ppermute(par, "member", [(i, i ^ (2 * d)) for i in range(members)])
                for d in others]
        par, made = lax.optimization_barrier((par, made))
        of_fine, of_coarse = made[:4], made[4:]
        par = jnp.concatenate([par, side_a[rows:, :LANES], side_b[rows:]] + more, axis=0)
        twin = lax.ppermute(par, "member", [(i, i ^ 1) for i in range(members)])

        groups = tiles * n_coarse * cz // LANES
        early = max(groups // 2, 1)
        part = jax.ShapeDtypeStruct((cx, cz, cy), jnp.float32)
        near, force = pl.pallas_call(
            functools.partial(coarse_near_kernel, tiles, range(early), coarse_sizes, n_fine,
                              n_coarse, (height, EDGE * 2, rows // cz)),
            out_shape=(part, level_shapes(cx, cy)[3]),
            in_specs=[VMEM] * 7,
            out_specs=(VMEM, VMEM),
            scratch_shapes=scratch(early, cx, cy, cx),
            compiler_params=limit(16),
            name="coarse_near",
        )(*of_coarse, source_coarse, par, side_a, side_b)

        fine_groups = tiles * n_fine * nz // LANES
        fine = pl.pallas_call(
            functools.partial(fine_kernel, tiles, fine_groups, fine_sizes, strip, n_fine),
            out_shape=jax.ShapeDtypeStruct((nx // 2, nz // 2, ny // 2), jnp.float32),
            in_specs=[VMEM] * 7 + [HBM],
            out_specs=VMEM,
            scratch_shapes=scratch(2 * fine_groups, nx, ny, nx // 2)
            + [pltpu.VMEM((REACH, height, LANES), jnp.float32)],
            compiler_params=limit(24),
            name="fine_smooth",
        )(*of_fine, par, twin, side_a, near)
        arrived = lax.ppermute(fine, axes, everywhere(owner))

        far = pl.pallas_call(
            functools.partial(coarse_far_kernel, tiles, range(early, groups), range(groups),
                              coarse_sizes, n_fine, n_coarse),
            out_shape=part,
            in_specs=[VMEM] * 7,
            out_specs=VMEM,
            scratch_shapes=scratch(2 * groups - early, cx, cy, cx),
            compiler_params=limit(16),
            name="coarse_far",
        )(*of_coarse, force, par, twin, near)
        return arrived + far

    return jax.shard_map(
        body,
        mesh=mesh,
        in_specs=(
            P("member", None), P("member", None), P("member"), P("member"),
            P(), P(), P(), P("tile", None, None), P(None, None, "tile"),
        ),
        out_specs=P("member", None, "tile"),
        check_vma=False,
    )
```

```python
import functools
import math

import jax
import jax.numpy as jnp
from jax import lax
from jax.experimental import pallas as pl
from jax.experimental.pallas import tpu as pltpu
from jax.sharding import PartitionSpec as P

NODES = 9
SWEEPS = 3
CENTRE = 1.125
HALF_WIDTH = 0.875
SPREAD_RATIO = CENTRE / HALF_WIDTH

LANES = 128
HALO = SWEEPS
REACH = SWEEPS - 1
EDGE = 4
PAD = 8
FAR = -2048.0
TERMS = 16
BLOCK = 8


def sweep_factors(sweep_count):
    previous = 1.0 / SPREAD_RATIO
    factors = []
    for _ in range(sweep_count - 1):
        current = 1.0 / (2.0 * SPREAD_RATIO - previous)
        factors.append((current * previous, 2.0 * current / HALF_WIDTH))
        previous = current
    return factors


(A1, B1), (A2, B2) = sweep_factors(SWEEPS)
FIRST = A1 / B1 + CENTRE - 1.0
KEEP0 = (1.0 - B2 * A1 / B1) / (B1 * B2)
KEEP1 = (1.0 + A2 + B2 / B1 - B2) / B2
SHIFT = 0.5 * (FIRST + KEEP1)
REST = KEEP0 + KEEP1 * FIRST - SHIFT * SHIFT
SCALE = 2.0 / CENTRE * B1 * B2 * SHIFT ** 3
EXACT = lax.Precision.HIGHEST
ROWS = (((0,), (0,)), ((), ()))
COLUMNS = (((1,), (1,)), ((), ()))


def iota(shape, dim):
    return lax.broadcasted_iota(jnp.int32, shape, dim)


def pieces(value):
    high = value.astype(jnp.bfloat16)
    rest = value - high.astype(jnp.float32)
    mid = rest.astype(jnp.bfloat16)
    low = (rest - mid.astype(jnp.float32)).astype(jnp.bfloat16)
    return high, mid, low


def aligned(at):
    return at if isinstance(at, int) else pl.multiple_of(at, 8)


def quarter(b, t, tiles):
    return b ^ t ^ jnp.where(t < tiles // 2, tiles - 1, 0)


class Place:
    def __init__(self, tiles):
        m, t = lax.axis_index("member"), lax.axis_index("tile")
        self.tiles, self.m, self.t = tiles, m, t
        self.a, self.b = m % 2, m // 2
        self.half = self.a ^ (t % 2)

    def beside(self, outward):
        step = jnp.where(self.half == 1, 1, -1)
        to = self.t + (step if outward else -step)
        return jnp.where((to >= 0) & (to < self.tiles), to, self.t)


def prep_kernel(tiles, nx, ny, cx, bits, terms, count, pk_ref, sf_ref, sc_hbm,
                a_ref, b_ref, par_ref, plane_ref, sc_ref, sems):
    here = Place(tiles)
    strip, nz, full_y = sf_ref.shape
    full_x, cz, cy = sc_hbm.shape
    height = ny + 2 * EDGE
    start = jnp.where(here.half == 1, strip - REACH, 0)
    copy = pltpu.make_async_copy(sf_ref.at[pl.ds(start, REACH)], plane_ref, sems.at[0])
    copy.start()
    window = cx + 2 * REACH
    lows = [jnp.clip(cx * ((here.b ^ bit) * 2 + here.a) - REACH, 0, full_x - window) for bit in bits]
    blocks = [pltpu.make_async_copy(sc_hbm.at[pl.ds(lows[k], window)], sc_ref.at[k], sems.at[1 + k])
              for k in range(2)]
    for item in blocks:
        item.start()

    packed = pk_ref[...]
    lane = iota(packed.shape, 1)
    row = iota(packed.shape, 0)
    weight = jnp.broadcast_to(packed[count:count + 1, :].astype(jnp.float32), packed.shape)
    weight = jnp.sum(jnp.where(lane == row, weight, 0.0), axis=1, keepdims=True)
    out = jnp.where((lane == terms) | (lane == terms + 1), 1.0, 0.0)
    out = jnp.where((lane == terms + 2) & (row < count), weight, out)
    for k in range(NODES):
        out = jnp.where((lane < terms) & (packed == k), math.cos(math.pi * k / (NODES - 1)), out)
    par_ref[...] = out

    rows = REACH * nz
    per_group = rows // cz
    spot = iota((rows, LANES), 1)

    for item in blocks:
        item.wait()

    def coarse_side(side, last, at):
        shifted = cx * ((here.b ^ bits[side]) * 2 + here.a) - REACH - lows[side]
        total = jnp.zeros((rows, LANES), jnp.float32)
        for group in range((cx + 2 * REACH) // per_group):
            parts = [sc_ref[side, jnp.clip(shifted + group * per_group + k, 0, window - 1)]
                     for k in range(per_group)]
            block = jnp.concatenate(parts, axis=0)
            block = jnp.concatenate([block] * (LANES // cy), axis=1)
            to = at + REACH * group
            shift = jnp.where(last, (to - cy + REACH) % LANES, to % LANES)
            block = pltpu.roll(block, shift, 1)
            total = jnp.where((spot >= to) & (spot < to + REACH), block, total)
        return total

    b_ref[0:rows, :] = coarse_side(1, here.half == 0, EDGE * 2)
    edge = coarse_side(0, here.half == 1, height % LANES)
    b_ref[rows:rows + BLOCK, :] = par_ref[...]
    a_ref[rows:rows + BLOCK, 0:LANES] = par_ref[...]

    target = quarter(here.b ^ bits[0], here.beside(True), tiles)
    shift = (EDGE + full_y - ny * target) % full_y
    copy.wait()
    for k in range(REACH):
        turned = pltpu.roll(plane_ref[k], shift, 1)
        part = slice(k * nz, (k + 1) * nz)
        for col in range(a_ref.shape[1] // LANES):
            block = turned[:, col * LANES:(col + 1) * LANES]
            if col == height // LANES:
                block = jnp.where(iota((nz, LANES), 1) < height % LANES, block, edge[part])
            a_ref[part, col * LANES:(col + 1) * LANES] = block


def factors(ratio, terms, nx, ny, nz, x0, y0, full_x, full_y, tx_ref, ty_ref,
            xb_ref, yt_ref, zt_ref):
    nxe, height = nx + 2 * HALO, ny + 2 * EDGE
    row = iota((TERMS, LANES), 0)
    xw = pltpu.roll(tx_ref[0], (ratio * (HALO - x0) + 2 * LANES) % LANES, 1)
    if ratio == 2:
        xw = 0.5 * (xw + pltpu.roll(xw, LANES - 1, 1))
    for i in range(nxe):
        at = x0 - HALO + i
        far = jnp.where((at < 0) | (at >= full_x), FAR, 0.0)
        col = jnp.broadcast_to(xw[:, ratio * i:ratio * i + 1], (TERMS, LANES))
        xb_ref[i] = jnp.where(row == terms, 1.0, jnp.where(row == terms + 1, far, col))
    span = -(-ratio * height // LANES) * LANES
    yw = pltpu.roll(ty_ref[...], (ratio * (EDGE - y0) + ratio * full_y) % (ratio * full_y), 1)
    yw = jnp.concatenate([yw[:, :span]] * 6, axis=0)
    pick = jnp.where(iota((height, span), 1) // ratio == iota((height, span), 0), 1.0 / ratio, 0.0)
    yt = lax.dot_general(pick, yw, COLUMNS, precision=EXACT, preferred_element_type=jnp.float32)
    lane = iota(yt.shape, 1)
    at = y0 - EDGE + iota(yt.shape, 0)
    far = jnp.where((at < 0) | (at >= full_y), FAR, 0.0)
    yt = jnp.where(lane % TERMS == terms, far, jnp.where(lane % TERMS == terms + 1, 1.0, yt))
    high, mid, low = (part.astype(jnp.float32) for part in pieces(yt))
    yt_ref[...] = jnp.where(lane < 3 * TERMS, high, jnp.where(lane < 5 * TERMS, mid, low)).astype(
        jnp.bfloat16)
    down, across = iota((LANES, LANES), 0), iota((LANES, LANES), 1)
    pick = jnp.where(down // ratio == across % nz, 1.0 / ratio, 0.0)
    zt = jnp.dot(tx_ref[1], pick, precision=EXACT, preferred_element_type=jnp.float32)
    zt_ref[...] = jnp.where((row == terms) | (row == terms + 1), 1.0, zt)


def members_of(pars, nz, first_row, per_device, zt_ref, yz_ref):
    weights = []
    for par_ref, groups in pars:
        size = par_ref.shape[0]
        for g in groups:
            member = (LANES // nz) * g + iota((size, LANES), 1) // nz
            source = BLOCK * (member // per_device) + first_row + member % per_device
            pick = jnp.where(iota((size, LANES), 0) == source, 1.0, 0.0)
            named = lax.dot_general(par_ref[:, 0:TERMS], pick, ROWS, precision=EXACT,
                                    preferred_element_type=jnp.float32)
            yz_ref[len(weights)] = named * zt_ref[...]
            weights.append(named[TERMS - 2:TERMS - 1, :])
    return weights


def chunks(count, run):
    for k in range(count):
        run(k)


def sweeps(groups, nx, ny, nz, x0, y0, full_x, full_y, pair, weights,
           xb_ref, yt_ref, yz_ref, force, c_ref, kz_ref, q_ref, d_ref, e_ref, u_ref, finish):
    nxe, height = nx + 2 * HALO, ny + 2 * EDGE

    def conduct(i, carry):
        row = xb_ref[i]
        for g in range(groups):
            high, middle, low = pieces(row * yz_ref[g])
            stacked = jnp.concatenate([high, middle, low, high, middle, high], axis=0)
            power = jnp.dot(yt_ref[...], stacked, preferred_element_type=jnp.float32)
            c_ref[g, i, pl.ds(PAD, height), :] = jnp.exp(power)
        return carry

    lax.fori_loop(0, nxe, conduct, 0, unroll=nxe)

    lane = iota((8, LANES), 1) % nz
    is_last, is_first = lane == nz - 1, lane == 0

    def start(k):
        at = aligned(PAD + 8 * k)
        here, up, down = pl.ds(at, 8), pl.ds(at + 1, 8), pl.ds(at - 1, 8)
        own = pl.ds(aligned(8 * k), 8)
        for g in range(groups):
            before, c0 = c_ref[g, 0, here, :], c_ref[g, 1, here, :]
            for i in range(1, nxe - 1):
                after = c_ref[g, i + 1, here, :]
                zp = jnp.where(is_last, 0.0, pltpu.roll(c0, LANES - 1, 1))
                zm = jnp.where(is_first, 0.0, pltpu.roll(c0, 1, 1))
                total = (6.0 * c0 + (before + after)) + (
                    (c_ref[g, i, up, :] + c_ref[g, i, down, :]) + (zp + zm))
                q = (1.0 / SHIFT) / total
                q_ref[g, i, here, :] = q
                d_ref[g, i, here, :] = force(i - 1, own) * q
                kz_ref[g, i, here, :] = jnp.where(is_last, 0.0, c0 + zp)
                before, c0 = c0, after

    chunks(height // 8, start)

    def clear_planes(planes):
        for g in range(groups):
            for i in planes:
                zero = jnp.zeros((height, LANES), jnp.float32)
                q_ref[g, i, pl.ds(PAD, height), :] = zero
                d_ref[g, i, pl.ds(PAD, height), :] = zero

    def clear_rows(at):
        for g in range(groups):
            for i in range(1, nxe - 1):
                zero = jnp.zeros((EDGE, LANES), jnp.float32)
                q_ref[g, i, pl.ds(PAD + at, EDGE), :] = zero
                d_ref[g, i, pl.ds(PAD + at, EDGE), :] = zero

    pl.when(x0 == 0)(lambda: clear_planes(range(1, HALO)))
    pl.when(x0 + nx == full_x)(lambda: clear_planes(range(nx + HALO, nxe - 1)))
    pl.when(y0 == 0)(lambda: clear_rows(0))
    pl.when(y0 + ny == full_y)(lambda: clear_rows(EDGE + ny))

    def walk(g, v_ref, first, last, here, up, down):
        c0, v0 = c_ref[g, first, here, :], v_ref[g, first, here, :]
        v_before = v_ref[g, first - 1, here, :]
        k_before = c_ref[g, first - 1, here, :] + c0
        for i in range(first, last):
            c_after, v_after = c_ref[g, i + 1, here, :], v_ref[g, i + 1, here, :]
            k_after = c0 + c_after
            kz = kz_ref[g, i, here, :]
            along_x = k_after * v_after + k_before * v_before
            along_y = ((c0 + c_ref[g, i, up, :]) * v_ref[g, i, up, :]
                       + (c0 + c_ref[g, i, down, :]) * v_ref[g, i, down, :])
            along_z = kz * pltpu.roll(v0, LANES - 1, 1) + pltpu.roll(kz * v0, 1, 1)
            yield i, v0 + q_ref[g, i, here, :] * ((along_x + along_y) + along_z)
            c0, v0, v_before, k_before = c_after, v_after, v0, k_after

    def first(k):
        at = aligned(PAD + 8 * k)
        here, up, down = pl.ds(at, 8), pl.ds(at + 1, 8), pl.ds(at - 1, 8)
        for g in range(groups):
            for i, value in walk(g, d_ref, 2, nxe - 2, here, up, down):
                e_ref[g, i, here, :] = value

    chunks(height // 8, first)

    step = 2 if pair else 1
    scale = SCALE * (0.125 if pair else 1.0)
    keep = REST / (SHIFT * SHIFT)

    def second(k):
        at = PAD + EDGE + 8 * k
        here, up, down = pl.ds(at, 8), pl.ds(at + 1, 8), pl.ds(at - 1, 8)
        out = [None] * (nx // step)
        for g in range(groups):
            gain = jnp.broadcast_to(scale * weights[g], (8, LANES))
            held = None
            for i, value in walk(g, e_ref, HALO, nx + HALO, here, up, down):
                value = value + keep * d_ref[g, i, here, :]
                j = i - HALO
                if j % step:
                    value = held + value
                held = value
                if j % step == step - 1:
                    value = gain * value
                    out[j // step] = value if g == 0 else out[j // step] + value
        for j, value in enumerate(out):
            u_ref[j, pl.ds(aligned(8 * k), 8), :] = value

    chunks(ny // 8, second)

    out_z = nz // step
    match = iota((out_z, 3 * LANES), 1) % nz // step == iota((out_z, 3 * LANES), 0)
    gather = jnp.where(match, 1.0, 0.0).astype(jnp.bfloat16)
    for j in range(nx // step):
        if pair:
            total = (u_ref[j, pl.ds(0, ny // 2, stride=2), :]
                     + u_ref[j, pl.ds(1, ny // 2, stride=2), :])
        else:
            total = u_ref[j]
        stacked = jnp.concatenate(pieces(total), axis=1)
        finish(j, lax.dot_general(gather, stacked, COLUMNS, preferred_element_type=jnp.float32))


def spread_of(nz):
    match = iota((3 * nz, LANES), 0) % nz == iota((3 * nz, LANES), 1) % nz
    return jnp.where(match, 1.0, 0.0).astype(jnp.bfloat16)


def force_of(source, spread):
    return lax.dot_general(jnp.concatenate(pieces(source), axis=0), spread, ROWS,
                           preferred_element_type=jnp.float32)


def fine_place(here, strip, nx, ny):
    return here.t * strip + here.half * nx, quarter(here.b, here.t, here.tiles) * ny


def table_kernel(tiles, fine_sizes, coarse_sizes, mx_ref, my_ref, mz_ref, sf_ref, order_ref,
                 fx_ref, fy_ref, fz_ref, ff_ref, cx_ref, cy_ref, cz_ref, tx_ref, ty_ref):
    here = Place(tiles)
    nx, ny, nz, full_x, full_y = fine_sizes
    strip = sf_ref.shape[0]
    count = nx + REACH
    terms = mx_ref.shape[0]
    tx_ref[...] = jnp.zeros_like(tx_ref)
    tx_ref[0, 0:terms, 0:mx_ref.shape[1]] = mx_ref[...]
    tx_ref[1, 0:terms, 0:mz_ref.shape[1]] = mz_ref[...]
    ty_ref[...] = jnp.zeros_like(ty_ref)
    ty_ref[0:terms, :] = my_ref[...]
    x0, y0 = fine_place(here, strip, nx, ny)
    factors(1, terms, nx, ny, nz, x0, y0, full_x, full_y, tx_ref, ty_ref, fx_ref, fy_ref, fz_ref)
    shift = (EDGE + full_y - y0) % full_y
    height = ff_ref.shape[1]
    spread = spread_of(nz)
    low = jnp.where(here.half == 0, 0, strip - count)
    for k in range(count):
        source = pltpu.roll(sf_ref[low + k], shift, 1)[:, :height]
        ff_ref[k + REACH * (1 - here.half)] = force_of(source, spread)

    nx, ny, nz, full_x, full_y = coarse_sizes
    factors(2, terms, nx, ny, nz, here.m * nx, here.t * ny, full_x, full_y, tx_ref, ty_ref,
            cx_ref, cy_ref, cz_ref)


def fine_kernel(tiles, groups, sizes, strip, per_device,
                x_ref, y_ref, z_ref, f_ref, one_ref, two_ref, side_ref, order_ref, out_ref,
                yz_ref, c_ref, kz_ref, q_ref, d_ref, e_ref, u_ref, edge_ref):
    here = Place(tiles)
    nx, ny, nz, full_x, full_y = sizes
    height = ny + 2 * EDGE
    x0, y0 = fine_place(here, strip, nx, ny)
    weights = members_of(((one_ref, range(groups)), (two_ref, range(groups))), nz, 0, per_device, z_ref, yz_ref)
    spread = spread_of(nz)
    for k in range(REACH):
        edge_ref[k] = force_of(side_ref[k * nz:(k + 1) * nz, :height], spread)
    count = nx + REACH

    def force(k, rows):
        if k < REACH:
            return jnp.where(here.half == 0, edge_ref[k, rows, :], f_ref[k, rows, :])
        if k >= count:
            return jnp.where(here.half == 0, f_ref[k, rows, :], edge_ref[k - count, rows, :])
        return f_ref[k, rows, :]

    def finish(j, value):
        out_ref[j] = value

    sweeps(2 * groups, nx, ny, nz, x0, y0, full_x, full_y, True, weights, x_ref, y_ref, yz_ref,
           force, c_ref, kz_ref, q_ref, d_ref, e_ref, u_ref, finish)


def coarse_sweeps(here, sizes, weights, x_ref, y_ref, f_ref, base_ref, out_ref,
                  yz_ref, c_ref, kz_ref, q_ref, d_ref, e_ref, u_ref):
    nx, ny, nz, full_x, full_y = sizes

    def finish(j, value):
        out_ref[j] = value if base_ref is None else base_ref[j] + value

    sweeps(len(weights), nx, ny, nz, here.m * nx, here.t * ny, full_x, full_y, False, weights,
           x_ref, y_ref, yz_ref, lambda k, rows: f_ref[k, rows, :], c_ref, kz_ref, q_ref, d_ref,
           e_ref, u_ref, finish)


def coarse_near_kernel(tiles, groups, sizes, first_row, per_device, side_at,
                       x_ref, y_ref, z_ref, sc_ref, par_ref, a_ref, b_ref, out_ref, full_ref,
                       yz_ref, *grids):
    here = Place(tiles)
    nx, ny, nz, full_x, _ = sizes
    spread = spread_of(nz)
    per_group = side_at[2]
    for k in range(nx + 2 * REACH):
        full_ref[k, 0:8, :] = jnp.zeros((8, LANES), jnp.float32)
        full_ref[k, ny:ny + 2 * EDGE, :] = jnp.zeros((8, LANES), jnp.float32)
        x = jnp.clip(here.m * nx - REACH + k, 0, full_x - 1)
        full_ref[k, EDGE:EDGE + ny, :] = force_of(sc_ref[x], spread)
        rows = slice(k % per_group * nz, (k % per_group + 1) * nz)
        found = []
        for ref, at in ((a_ref, side_at[0]), (b_ref, side_at[1])):
            low = at // 16 * 16
            block = force_of(ref[rows, low:low + 16], spread)
            at = at - low + REACH * (k // per_group)
            found.append(block[at:at + REACH])
        full_ref[k, EDGE - REACH:EDGE, :] = jnp.where(here.half == 0, found[0], found[1])
        full_ref[k, EDGE + ny:EDGE + ny + REACH, :] = jnp.where(
            here.half == 0, found[1], found[0])
    weights = members_of(((par_ref, groups),), nz, first_row, per_device, z_ref, yz_ref)
    coarse_sweeps(here, sizes, weights, x_ref, y_ref, full_ref, None, out_ref, yz_ref, *grids)


def coarse_far_kernel(tiles, groups, twin_groups, sizes, first_row, per_device,
                      x_ref, y_ref, z_ref, f_ref, par_ref, twin_ref, base_ref, out_ref,
                      yz_ref, *grids):
    here = Place(tiles)
    weights = members_of(((par_ref, groups), (twin_ref, twin_groups)), sizes[2], first_row,
                         per_device, z_ref, yz_ref)
    coarse_sweeps(here, sizes, weights, x_ref, y_ref, f_ref, base_ref, out_ref, yz_ref, *grids)


def scratch(groups, nx, ny, count):
    nxe, height = nx + 2 * HALO, ny + 2 * EDGE
    grid = pltpu.VMEM((groups, nxe, height + 2 * PAD, LANES), jnp.float32)
    return [pltpu.VMEM((groups, TERMS, LANES), jnp.float32), grid, grid, grid, grid, grid,
            pltpu.VMEM((count, ny, LANES), jnp.float32)]


def level_shapes(nx, ny):
    nxe, height = nx + 2 * HALO, ny + 2 * EDGE
    return (jax.ShapeDtypeStruct((nxe, TERMS, LANES), jnp.float32),
            jax.ShapeDtypeStruct((height, 6 * TERMS), jnp.bfloat16),
            jax.ShapeDtypeStruct((TERMS, LANES), jnp.float32),
            jax.ShapeDtypeStruct((nx + 2 * REACH, height, LANES), jnp.float32))


def limit(mebibytes):
    return pltpu.CompilerParams(vmem_limit_bytes=mebibytes << 20)


VMEM = pl.BlockSpec(memory_space=pltpu.VMEM)
SMEM = pl.BlockSpec(memory_space=pltpu.SMEM)
HBM = pl.BlockSpec(memory_space=pl.ANY)
FIXED = pl.BlockSpec(memory_space=pltpu.HBM)


def solution(mesh):
    members, tiles = mesh.shape["member"], mesh.shape["tile"]
    assert members == 2 * tiles and tiles >= 4
    axes = ("member", "tile")
    bits = (tiles // 2, tiles // 4)
    others = [d for d in range(1, tiles) if d not in bits]

    def flat(b, a, t):
        return (b * 2 + a) * tiles + t

    def everywhere(rule):
        return [(flat(b, a, t), flat(*rule(b, a, t)))
                for b in range(tiles) for a in range(2) for t in range(tiles)]

    def beside(bit, outward):
        def rule(b, a, t):
            step = 1 if a ^ (t % 2) else -1
            to = t + (step if outward else -step)
            return b ^ bit, a, to if 0 <= to < tiles else t
        return everywhere(rule)

    def owner(b, a, t):
        return t, a ^ (t % 2), b ^ t ^ (tiles - 1 if t < tiles // 2 else 0)

    def body(node_fine, node_coarse, weight_fine, weight_coarse, mode_x, mode_y, mode_z,
             source_fine, source_coarse):
        strip, nz, full_y = source_fine.shape
        full_cx, cz, cy = source_coarse.shape
        full_x = mode_x.shape[1]
        nx, ny, cx = full_x // members, full_y // tiles, full_cx // members
        n_fine, n_coarse = node_fine.shape[0], node_coarse.shape[0]
        height = ny + 2 * EDGE
        rows = REACH * nz
        width = -(-(height + REACH * 2) // LANES) * LANES
        fine_sizes = nx, ny, nz, full_x, full_y
        coarse_sizes = cx, cy, cz, full_cx, cy * tiles

        terms, count = mode_x.shape[0], n_fine + n_coarse
        packed = (
            jnp.pad(node_fine, ((0, BLOCK - n_fine), (0, LANES - terms)))
            + jnp.pad(node_coarse, ((n_fine, BLOCK - count), (0, LANES - terms)))
            + jnp.pad(weight_fine[None, :], ((count, BLOCK - count - 1), (0, LANES - n_fine)))
            + jnp.pad(weight_coarse[None, :],
                      ((count, BLOCK - count - 1), (n_fine, LANES - count))))
        side_a, side_b, par = pl.pallas_call(
            functools.partial(prep_kernel, tiles, nx, ny, cx, bits, terms, count),
            out_shape=(jax.ShapeDtypeStruct((rows + BLOCK, width), jnp.float32),
                       jax.ShapeDtypeStruct((rows + BLOCK, LANES), jnp.float32),
                       jax.ShapeDtypeStruct((BLOCK, LANES), jnp.float32)),
            in_specs=[VMEM, HBM, HBM],
            out_specs=(VMEM, VMEM, VMEM),
            scratch_shapes=[pltpu.VMEM((REACH, nz, full_y), jnp.float32),
                            pltpu.VMEM((2, cx + 2 * REACH, cz, cy), jnp.float32),
                            pltpu.SemaphoreType.DMA((3,))],
            compiler_params=pltpu.CompilerParams(vmem_limit_bytes=67043328 - (10480 << 10)),
            name="prep",
        )(packed, source_fine, source_coarse)

        made = pl.pallas_call(
            functools.partial(table_kernel, tiles, fine_sizes, coarse_sizes),
            out_shape=level_shapes(nx, ny) + level_shapes(cx, cy)[:3],
            in_specs=[VMEM] * 4 + [HBM],
            out_specs=(VMEM,) * 7,
            scratch_shapes=[pltpu.VMEM((2, TERMS, LANES), jnp.float32),
                            pltpu.VMEM((TERMS, full_y), jnp.float32)],
            compiler_params=limit(8),
            name="tables",
        )(mode_x, mode_y, mode_z, source_fine, par)

        side_a = lax.ppermute(side_a, axes, beside(bits[0], True))
        side_b = lax.ppermute(side_b, axes, beside(bits[1], False))
        more = [lax.ppermute(par, "member", [(i, i ^ (2 * d)) for i in range(members)])
                for d in others]
        par, made = lax.optimization_barrier((par, made))
        of_fine, of_coarse = made[:4], made[4:]
        par = jnp.concatenate([par, side_a[rows:, :LANES], side_b[rows:]] + more, axis=0)
        twin = lax.ppermute(par, "member", [(i, i ^ 1) for i in range(members)])

        groups = tiles * n_coarse * cz // LANES
        early = max(groups // 2, 1)
        part = jax.ShapeDtypeStruct((cx, cz, cy), jnp.float32)
        near, force = pl.pallas_call(
            functools.partial(coarse_near_kernel, tiles, range(early), coarse_sizes, n_fine,
                              n_coarse, (height, EDGE * 2, rows // cz)),
            out_shape=(part, level_shapes(cx, cy)[3]),
            in_specs=[VMEM] * 7,
            out_specs=(VMEM, VMEM),
            scratch_shapes=scratch(early, cx, cy, cx),
            compiler_params=limit(16),
            name="coarse_near",
        )(*of_coarse, source_coarse, par, side_a, side_b)

        fine_groups = tiles * n_fine * nz // LANES
        fine = pl.pallas_call(
            functools.partial(fine_kernel, tiles, fine_groups, fine_sizes, strip, n_fine),
            out_shape=jax.ShapeDtypeStruct((nx // 2, nz // 2, ny // 2), jnp.float32),
            in_specs=[VMEM] * 7 + [HBM],
            out_specs=VMEM,
            scratch_shapes=scratch(2 * fine_groups, nx, ny, nx // 2)
            + [pltpu.VMEM((REACH, height, LANES), jnp.float32)],
            compiler_params=limit(24),
            name="fine_smooth",
        )(*of_fine, par, twin, side_a, near)
        arrived = lax.ppermute(fine, axes, everywhere(owner))

        far = pl.pallas_call(
            functools.partial(coarse_far_kernel, tiles, range(early, groups), range(groups),
                              coarse_sizes, n_fine, n_coarse),
            out_shape=part,
            in_specs=[VMEM] * 7,
            out_specs=VMEM,
            scratch_shapes=scratch(2 * groups - early, cx, cy, cx),
            compiler_params=limit(16),
            name="coarse_far",
        )(*of_coarse, force, par, twin, near)
        return arrived + far

    return jax.shard_map(
        body,
        mesh=mesh,
        in_specs=(
            P("member", None), P("member", None), P("member"), P("member"),
            P(), P(), P(), P("tile", None, None), P(None, None, "tile"),
        ),
        out_specs=P("member", None, "tile"),
        check_vma=False,
    )
```

```python
import functools
import math

import jax
import jax.numpy as jnp
from jax import lax
from jax.experimental import pallas as pl
from jax.experimental.pallas import tpu as pltpu
from jax.sharding import PartitionSpec as P


NODES = 9
SWEEPS = 3
CENTRE = 1.125
HALF_WIDTH = 0.875
SPREAD_RATIO = CENTRE / HALF_WIDTH

LANES = 128
HALO = SWEEPS
REACH = SWEEPS - 1
EDGE = 4
PAD = 8
FAR = -2048.0
TERMS = 16
BLOCK = 8


def sweep_factors(sweep_count):
    previous = 1.0 / SPREAD_RATIO
    factors = []
    for _ in range(sweep_count - 1):
        current = 1.0 / (2.0 * SPREAD_RATIO - previous)
        factors.append((current * previous, 2.0 * current / HALF_WIDTH))
        previous = current
    return factors


(A1, B1), (A2, B2) = sweep_factors(SWEEPS)
FIRST = A1 / B1 + CENTRE - 1.0
KEEP0 = (1.0 - B2 * A1 / B1) / (B1 * B2)
KEEP1 = (1.0 + A2 + B2 / B1 - B2) / B2
SHIFT = 0.5 * (FIRST + KEEP1)
REST = KEEP0 + KEEP1 * FIRST - SHIFT * SHIFT
SCALE = 2.0 / CENTRE * B1 * B2 * SHIFT ** 3
EXACT = lax.Precision.HIGHEST
ROWS = (((0,), (0,)), ((), ()))
COLUMNS = (((1,), (1,)), ((), ()))


def iota(shape, dim):
    return lax.broadcasted_iota(jnp.int32, shape, dim)


def pieces(value):
    high = value.astype(jnp.bfloat16)
    rest = value - high.astype(jnp.float32)
    mid = rest.astype(jnp.bfloat16)
    low = (rest - mid.astype(jnp.float32)).astype(jnp.bfloat16)
    return high, mid, low


def aligned(at):
    return at if isinstance(at, int) else pl.multiple_of(at, 8)


def quarter(b, t, tiles):
    return b ^ t ^ jnp.where(t < tiles // 2, tiles - 1, 0)


class Place:
    def __init__(self, tiles):
        m, t = lax.axis_index("member"), lax.axis_index("tile")
        self.tiles, self.m, self.t = tiles, m, t
        self.a, self.b = m % 2, m // 2
        self.half = self.a ^ (t % 2)

    def beside(self, outward):
        step = jnp.where(self.half == 1, 1, -1)
        to = self.t + (step if outward else -step)
        return jnp.where((to >= 0) & (to < self.tiles), to, self.t)


def prep_kernel(tiles, ny, cx, bits, terms, count, pk_ref, sf_ref, sc_hbm,
                a_ref, b_ref, par_ref, plane_ref, sc_ref, sems):
    here = Place(tiles)
    strip, nz, full_y = sf_ref.shape
    full_x, cz, cy = sc_hbm.shape
    height = ny + 2 * EDGE
    start = jnp.where(here.half == 1, strip - REACH, 0)
    copy = pltpu.make_async_copy(sf_ref.at[pl.ds(start, REACH)], plane_ref, sems.at[0])
    copy.start()
    window = cx + 2 * REACH
    lows = [jnp.clip(cx * ((here.b ^ bit) * 2 + here.a) - REACH, 0, full_x - window) for bit in bits]
    blocks = [pltpu.make_async_copy(sc_hbm.at[pl.ds(lows[k], window)], sc_ref.at[k], sems.at[1 + k])
              for k in range(2)]
    for item in blocks:
        item.start()

    packed = pk_ref[...]
    lane = iota(packed.shape, 1)
    row = iota(packed.shape, 0)
    weight = jnp.broadcast_to(packed[count:count + 1, :].astype(jnp.float32), packed.shape)
    weight = jnp.sum(jnp.where(lane == row, weight, 0.0), axis=1, keepdims=True)
    out = jnp.where((lane == terms) | (lane == terms + 1), 1.0, 0.0)
    out = jnp.where((lane == terms + 2) & (row < count), weight, out)
    for k in range(NODES):
        out = jnp.where((lane < terms) & (packed == k), math.cos(math.pi * k / (NODES - 1)), out)
    par_ref[...] = out

    rows = REACH * nz
    per_group = rows // cz
    spot = iota((rows, LANES), 1)

    for item in blocks:
        item.wait()

    def coarse_side(side, last, at):
        shifted = cx * ((here.b ^ bits[side]) * 2 + here.a) - REACH - lows[side]
        total = jnp.zeros((rows, LANES), jnp.float32)
        for group in range((cx + 2 * REACH) // per_group):
            parts = [sc_ref[side, jnp.clip(shifted + group * per_group + k, 0, window - 1)]
                     for k in range(per_group)]
            block = jnp.concatenate(parts, axis=0)
            block = jnp.concatenate([block] * (LANES // cy), axis=1)
            to = at + REACH * group
            shift = jnp.where(last, (to - cy + REACH) % LANES, to % LANES)
            block = pltpu.roll(block, shift, 1)
            total = jnp.where((spot >= to) & (spot < to + REACH), block, total)
        return total

    b_ref[0:rows, :] = coarse_side(1, here.half == 0, EDGE * 2)
    edge = coarse_side(0, here.half == 1, height % LANES)
    b_ref[rows:rows + BLOCK, :] = par_ref[...]
    a_ref[rows:rows + BLOCK, 0:LANES] = par_ref[...]

    target = quarter(here.b ^ bits[0], here.beside(True), tiles)
    shift = (EDGE + full_y - ny * target) % full_y
    copy.wait()
    for k in range(REACH):
        turned = pltpu.roll(plane_ref[k], shift, 1)
        part = slice(k * nz, (k + 1) * nz)
        for col in range(a_ref.shape[1] // LANES):
            block = turned[:, col * LANES:(col + 1) * LANES]
            if col == height // LANES:
                block = jnp.where(iota((nz, LANES), 1) < height % LANES, block, edge[part])
            a_ref[part, col * LANES:(col + 1) * LANES] = block


def factors(ratio, terms, nx, ny, nz, x0, y0, full_x, full_y, tx_ref, ty_ref,
            xb_ref, yt_ref, zt_ref):
    nxe, height = nx + 2 * HALO, ny + 2 * EDGE
    row = iota((TERMS, LANES), 0)
    xw = pltpu.roll(tx_ref[0], (ratio * (HALO - x0) + 2 * LANES) % LANES, 1)
    if ratio == 2:
        xw = 0.5 * (xw + pltpu.roll(xw, LANES - 1, 1))
    for i in range(nxe):
        at = x0 - HALO + i
        far = jnp.where((at < 0) | (at >= full_x), FAR, 0.0)
        col = jnp.broadcast_to(xw[:, ratio * i:ratio * i + 1], (TERMS, LANES))
        xb_ref[i] = jnp.where(row == terms, 1.0, jnp.where(row == terms + 1, far, col))
    span = -(-ratio * height // LANES) * LANES
    yw = pltpu.roll(ty_ref[...], (ratio * (EDGE - y0) + ratio * full_y) % (ratio * full_y), 1)
    yw = jnp.concatenate([yw[:, :span]] * 6, axis=0)
    pick = jnp.where(iota((height, span), 1) // ratio == iota((height, span), 0), 1.0 / ratio, 0.0)
    yt = lax.dot_general(pick, yw, COLUMNS, precision=EXACT, preferred_element_type=jnp.float32)
    lane = iota(yt.shape, 1)
    at = y0 - EDGE + iota(yt.shape, 0)
    far = jnp.where((at < 0) | (at >= full_y), FAR, 0.0)
    yt = jnp.where(lane % TERMS == terms, far, jnp.where(lane % TERMS == terms + 1, 1.0, yt))
    high, mid, low = (part.astype(jnp.float32) for part in pieces(yt))
    yt_ref[...] = jnp.where(lane < 3 * TERMS, high, jnp.where(lane < 5 * TERMS, mid, low)).astype(
        jnp.bfloat16)
    down, across = iota((LANES, LANES), 0), iota((LANES, LANES), 1)
    pick = jnp.where(down // ratio == across % nz, 1.0 / ratio, 0.0)
    zt = jnp.dot(tx_ref[1], pick, precision=EXACT, preferred_element_type=jnp.float32)
    zt_ref[...] = jnp.where((row == terms) | (row == terms + 1), 1.0, zt)


def members_of(pars, nz, first_row, per_device, zt_ref, yz_ref):
    weights = []
    for par_ref, groups in pars:
        size = par_ref.shape[0]
        for g in groups:
            member = (LANES // nz) * g + iota((size, LANES), 1) // nz
            source = BLOCK * (member // per_device) + first_row + member % per_device
            pick = jnp.where(iota((size, LANES), 0) == source, 1.0, 0.0)
            named = lax.dot_general(par_ref[:, 0:TERMS], pick, ROWS, precision=EXACT,
                                    preferred_element_type=jnp.float32)
            yz_ref[len(weights)] = named * zt_ref[...]
            weights.append(named[TERMS - 2:TERMS - 1, :])
    return weights


def chunks(count, run):
    for k in range(count):
        run(k)


def sweeps(groups, nx, ny, nz, x0, y0, full_x, full_y, pair, weights,
           xb_ref, yt_ref, yz_ref, force, c_ref, kz_ref, q_ref, d_ref, e_ref, u_ref, finish):
    nxe, height = nx + 2 * HALO, ny + 2 * EDGE

    def conduct(i, carry):
        row = xb_ref[i]
        for g in range(groups):
            high, middle, low = pieces(row * yz_ref[g])
            stacked = jnp.concatenate([high, middle, low, high, middle, high], axis=0)
            power = jnp.dot(yt_ref[...], stacked, preferred_element_type=jnp.float32)
            c_ref[g, i, pl.ds(PAD, height), :] = jnp.exp(power)
        return carry

    lax.fori_loop(0, nxe, conduct, 0, unroll=nxe)

    lane = iota((8, LANES), 1) % nz
    is_last, is_first = lane == nz - 1, lane == 0

    def start(k):
        at = aligned(PAD + 8 * k)
        here, up, down = pl.ds(at, 8), pl.ds(at + 1, 8), pl.ds(at - 1, 8)
        own = pl.ds(aligned(8 * k), 8)
        for g in range(groups):
            before, c0 = c_ref[g, 0, here, :], c_ref[g, 1, here, :]
            for i in range(1, nxe - 1):
                after = c_ref[g, i + 1, here, :]
                zp = jnp.where(is_last, 0.0, pltpu.roll(c0, LANES - 1, 1))
                zm = jnp.where(is_first, 0.0, pltpu.roll(c0, 1, 1))
                total = (6.0 * c0 + (before + after)) + (
                    (c_ref[g, i, up, :] + c_ref[g, i, down, :]) + (zp + zm))
                q = (1.0 / SHIFT) / total
                q_ref[g, i, here, :] = q
                d_ref[g, i, here, :] = force(i - 1, own) * q
                kz_ref[g, i, here, :] = jnp.where(is_last, 0.0, c0 + zp)
                before, c0 = c0, after

    chunks(height // 8, start)

    def clear_planes(planes):
        for g in range(groups):
            for i in planes:
                zero = jnp.zeros((height, LANES), jnp.float32)
                q_ref[g, i, pl.ds(PAD, height), :] = zero
                d_ref[g, i, pl.ds(PAD, height), :] = zero

    def clear_rows(at):
        for g in range(groups):
            for i in range(1, nxe - 1):
                zero = jnp.zeros((EDGE, LANES), jnp.float32)
                q_ref[g, i, pl.ds(PAD + at, EDGE), :] = zero
                d_ref[g, i, pl.ds(PAD + at, EDGE), :] = zero

    pl.when(x0 == 0)(lambda: clear_planes(range(1, HALO)))
    pl.when(x0 + nx == full_x)(lambda: clear_planes(range(nx + HALO, nxe - 1)))
    pl.when(y0 == 0)(lambda: clear_rows(0))
    pl.when(y0 + ny == full_y)(lambda: clear_rows(EDGE + ny))

    def walk(g, v_ref, first, last, here, up, down):
        c0, v0 = c_ref[g, first, here, :], v_ref[g, first, here, :]
        v_before = v_ref[g, first - 1, here, :]
        k_before = c_ref[g, first - 1, here, :] + c0
        for i in range(first, last):
            c_after, v_after = c_ref[g, i + 1, here, :], v_ref[g, i + 1, here, :]
            k_after = c0 + c_after
            kz = kz_ref[g, i, here, :]
            along_x = k_after * v_after + k_before * v_before
            along_y = ((c0 + c_ref[g, i, up, :]) * v_ref[g, i, up, :]
                       + (c0 + c_ref[g, i, down, :]) * v_ref[g, i, down, :])
            along_z = kz * pltpu.roll(v0, LANES - 1, 1) + pltpu.roll(kz * v0, 1, 1)
            yield i, v0 + q_ref[g, i, here, :] * ((along_x + along_y) + along_z)
            c0, v0, v_before, k_before = c_after, v_after, v0, k_after

    def first(k):
        at = aligned(PAD + 8 * k)
        here, up, down = pl.ds(at, 8), pl.ds(at + 1, 8), pl.ds(at - 1, 8)
        for g in range(groups):
            for i, value in walk(g, d_ref, 2, nxe - 2, here, up, down):
                e_ref[g, i, here, :] = value

    chunks(height // 8, first)

    step = 2 if pair else 1
    scale = SCALE * (0.125 if pair else 1.0)
    keep = REST / (SHIFT * SHIFT)

    def second(k):
        at = PAD + EDGE + 8 * k
        here, up, down = pl.ds(at, 8), pl.ds(at + 1, 8), pl.ds(at - 1, 8)
        out = [None] * (nx // step)
        for g in range(groups):
            gain = jnp.broadcast_to(scale * weights[g], (8, LANES))
            held = None
            for i, value in walk(g, e_ref, HALO, nx + HALO, here, up, down):
                value = value + keep * d_ref[g, i, here, :]
                j = i - HALO
                if j % step:
                    value = held + value
                held = value
                if j % step == step - 1:
                    value = gain * value
                    out[j // step] = value if g == 0 else out[j // step] + value
        for j, value in enumerate(out):
            u_ref[j, pl.ds(aligned(8 * k), 8), :] = value

    chunks(ny // 8, second)

    out_z = nz // step
    match = iota((out_z, 3 * LANES), 1) % nz // step == iota((out_z, 3 * LANES), 0)
    gather = jnp.where(match, 1.0, 0.0).astype(jnp.bfloat16)
    for j in range(nx // step):
        if pair:
            total = (u_ref[j, pl.ds(0, ny // 2, stride=2), :]
                     + u_ref[j, pl.ds(1, ny // 2, stride=2), :])
        else:
            total = u_ref[j]
        stacked = jnp.concatenate(pieces(total), axis=1)
        finish(j, lax.dot_general(gather, stacked, COLUMNS, preferred_element_type=jnp.float32))


def spread_of(nz):
    match = iota((3 * nz, LANES), 0) % nz == iota((3 * nz, LANES), 1) % nz
    return jnp.where(match, 1.0, 0.0).astype(jnp.bfloat16)


def force_of(source, spread):
    return lax.dot_general(jnp.concatenate(pieces(source), axis=0), spread, ROWS,
                           preferred_element_type=jnp.float32)


def fine_place(here, strip, nx, ny):
    return here.t * strip + here.half * nx, quarter(here.b, here.t, here.tiles) * ny


def table_kernel(tiles, fine_sizes, coarse_sizes, mx_ref, my_ref, mz_ref, sf_ref, order_ref,
                 fx_ref, fy_ref, fz_ref, ff_ref, cx_ref, cy_ref, cz_ref, tx_ref, ty_ref):
    here = Place(tiles)
    nx, ny, nz, full_x, full_y = fine_sizes
    strip = sf_ref.shape[0]
    count = nx + REACH
    terms = mx_ref.shape[0]
    tx_ref[...] = jnp.zeros_like(tx_ref)
    tx_ref[0, 0:terms, 0:mx_ref.shape[1]] = mx_ref[...]
    tx_ref[1, 0:terms, 0:mz_ref.shape[1]] = mz_ref[...]
    ty_ref[...] = jnp.zeros_like(ty_ref)
    ty_ref[0:terms, :] = my_ref[...]
    x0, y0 = fine_place(here, strip, nx, ny)
    factors(1, terms, nx, ny, nz, x0, y0, full_x, full_y, tx_ref, ty_ref, fx_ref, fy_ref, fz_ref)
    shift = (EDGE + full_y - y0) % full_y
    height = ff_ref.shape[1]
    spread = spread_of(nz)
    low = jnp.where(here.half == 0, 0, strip - count)
    for k in range(count):
        source = pltpu.roll(sf_ref[low + k], shift, 1)[:, :height]
        ff_ref[k + REACH * (1 - here.half)] = force_of(source, spread)

    nx, ny, nz, full_x, full_y = coarse_sizes
    factors(2, terms, nx, ny, nz, here.m * nx, here.t * ny, full_x, full_y, tx_ref, ty_ref,
            cx_ref, cy_ref, cz_ref)


def fine_kernel(tiles, groups, sizes, strip, per_device,
                x_ref, y_ref, z_ref, f_ref, one_ref, two_ref, side_ref, order_ref, out_ref,
                yz_ref, c_ref, kz_ref, q_ref, d_ref, e_ref, u_ref, edge_ref):
    here = Place(tiles)
    nx, ny, nz, full_x, full_y = sizes
    height = ny + 2 * EDGE
    x0, y0 = fine_place(here, strip, nx, ny)
    weights = members_of(((one_ref, range(groups)), (two_ref, range(groups))), nz, 0, per_device, z_ref, yz_ref)
    spread = spread_of(nz)
    for k in range(REACH):
        edge_ref[k] = force_of(side_ref[k * nz:(k + 1) * nz, :height], spread)
    count = nx + REACH

    def force(k, rows):
        if k < REACH:
            return jnp.where(here.half == 0, edge_ref[k, rows, :], f_ref[k, rows, :])
        if k >= count:
            return jnp.where(here.half == 0, f_ref[k, rows, :], edge_ref[k - count, rows, :])
        return f_ref[k, rows, :]

    def finish(j, value):
        out_ref[j] = value

    sweeps(2 * groups, nx, ny, nz, x0, y0, full_x, full_y, True, weights, x_ref, y_ref, yz_ref,
           force, c_ref, kz_ref, q_ref, d_ref, e_ref, u_ref, finish)


def coarse_sweeps(here, sizes, weights, x_ref, y_ref, f_ref, base_ref, out_ref,
                  yz_ref, c_ref, kz_ref, q_ref, d_ref, e_ref, u_ref):
    nx, ny, nz, full_x, full_y = sizes

    def finish(j, value):
        out_ref[j] = value if base_ref is None else base_ref[j] + value

    sweeps(len(weights), nx, ny, nz, here.m * nx, here.t * ny, full_x, full_y, False, weights,
           x_ref, y_ref, yz_ref, lambda k, rows: f_ref[k, rows, :], c_ref, kz_ref, q_ref, d_ref,
           e_ref, u_ref, finish)


def coarse_near_kernel(tiles, groups, sizes, first_row, per_device, side_at,
                       x_ref, y_ref, z_ref, sc_ref, par_ref, a_ref, b_ref, out_ref, full_ref,
                       yz_ref, *grids):
    here = Place(tiles)
    nx, ny, nz, full_x, _ = sizes
    spread = spread_of(nz)
    per_group = side_at[2]
    for k in range(nx + 2 * REACH):
        full_ref[k, 0:8, :] = jnp.zeros((8, LANES), jnp.float32)
        full_ref[k, ny:ny + 2 * EDGE, :] = jnp.zeros((8, LANES), jnp.float32)
        x = jnp.clip(here.m * nx - REACH + k, 0, full_x - 1)
        full_ref[k, EDGE:EDGE + ny, :] = force_of(sc_ref[x], spread)
        rows = slice(k % per_group * nz, (k % per_group + 1) * nz)
        found = []
        for ref, at in ((a_ref, side_at[0]), (b_ref, side_at[1])):
            low = at // 16 * 16
            block = force_of(ref[rows, low:low + 16], spread)
            at = at - low + REACH * (k // per_group)
            found.append(block[at:at + REACH])
        full_ref[k, EDGE - REACH:EDGE, :] = jnp.where(here.half == 0, found[0], found[1])
        full_ref[k, EDGE + ny:EDGE + ny + REACH, :] = jnp.where(
            here.half == 0, found[1], found[0])
    weights = members_of(((par_ref, groups),), nz, first_row, per_device, z_ref, yz_ref)
    coarse_sweeps(here, sizes, weights, x_ref, y_ref, full_ref, None, out_ref, yz_ref, *grids)


def coarse_far_kernel(tiles, groups, twin_groups, sizes, first_row, per_device,
                      x_ref, y_ref, z_ref, f_ref, par_ref, twin_ref, base_ref, out_ref,
                      yz_ref, *grids):
    here = Place(tiles)
    weights = members_of(((par_ref, groups), (twin_ref, twin_groups)), sizes[2], first_row,
                         per_device, z_ref, yz_ref)
    coarse_sweeps(here, sizes, weights, x_ref, y_ref, f_ref, base_ref, out_ref, yz_ref, *grids)


def scratch(groups, nx, ny, count):
    nxe, height = nx + 2 * HALO, ny + 2 * EDGE
    grid = pltpu.VMEM((groups, nxe, height + 2 * PAD, LANES), jnp.float32)
    return [pltpu.VMEM((groups, TERMS, LANES), jnp.float32), grid, grid, grid, grid, grid,
            pltpu.VMEM((count, ny, LANES), jnp.float32)]


def level_shapes(nx, ny):
    nxe, height = nx + 2 * HALO, ny + 2 * EDGE
    return (jax.ShapeDtypeStruct((nxe, TERMS, LANES), jnp.float32),
            jax.ShapeDtypeStruct((height, 6 * TERMS), jnp.bfloat16),
            jax.ShapeDtypeStruct((TERMS, LANES), jnp.float32),
            jax.ShapeDtypeStruct((nx + 2 * REACH, height, LANES), jnp.float32))


def limit(mebibytes):
    return pltpu.CompilerParams(vmem_limit_bytes=mebibytes << 20)


VMEM = pl.BlockSpec(memory_space=pltpu.VMEM)
SMEM = pl.BlockSpec(memory_space=pltpu.SMEM)
HBM = pl.BlockSpec(memory_space=pl.ANY)
FIXED = pl.BlockSpec(memory_space=pltpu.HBM)


def solution(mesh):
    members, tiles = mesh.shape["member"], mesh.shape["tile"]
    assert members == 2 * tiles and tiles >= 4
    axes = ("member", "tile")
    bits = (tiles // 2, tiles // 4)
    others = [d for d in range(1, tiles) if d not in bits]

    def flat(b, a, t):
        return (b * 2 + a) * tiles + t

    def everywhere(rule):
        return [(flat(b, a, t), flat(*rule(b, a, t)))
                for b in range(tiles) for a in range(2) for t in range(tiles)]

    def beside(bit, outward):
        def rule(b, a, t):
            step = 1 if a ^ (t % 2) else -1
            to = t + (step if outward else -step)
            return b ^ bit, a, to if 0 <= to < tiles else t

        return everywhere(rule)

    def owner(b, a, t):
        return t, a ^ (t % 2), b ^ t ^ (tiles - 1 if t < tiles // 2 else 0)

    def body(node_fine, node_coarse, weight_fine, weight_coarse, mode_x, mode_y, mode_z,
             source_fine, source_coarse):
        strip, nz, full_y = source_fine.shape
        full_cx, cz, cy = source_coarse.shape
        full_x = mode_x.shape[1]
        nx, ny, cx = full_x // members, full_y // tiles, full_cx // members
        n_fine, n_coarse = node_fine.shape[0], node_coarse.shape[0]
        height = ny + 2 * EDGE
        rows = REACH * nz
        width = -(-(height + REACH * 2) // LANES) * LANES
        fine_sizes = nx, ny, nz, full_x, full_y
        coarse_sizes = cx, cy, cz, full_cx, cy * tiles

        terms, count = mode_x.shape[0], n_fine + n_coarse
        packed = (
            jnp.pad(node_fine, ((0, BLOCK - n_fine), (0, LANES - terms)))
            + jnp.pad(node_coarse, ((n_fine, BLOCK - count), (0, LANES - terms)))
            + jnp.pad(weight_fine[None, :], ((count, BLOCK - count - 1), (0, LANES - n_fine)))
            + jnp.pad(weight_coarse[None, :],
                      ((count, BLOCK - count - 1), (n_fine, LANES - count))))
        side_a, side_b, par = pl.pallas_call(
            functools.partial(prep_kernel, tiles, ny, cx, bits, terms, count),
            out_shape=(jax.ShapeDtypeStruct((rows + BLOCK, width), jnp.float32),
                       jax.ShapeDtypeStruct((rows + BLOCK, LANES), jnp.float32),
                       jax.ShapeDtypeStruct((BLOCK, LANES), jnp.float32)),
            in_specs=[VMEM, HBM, HBM],
            out_specs=(VMEM, VMEM, VMEM),
            scratch_shapes=[pltpu.VMEM((REACH, nz, full_y), jnp.float32),
                            pltpu.VMEM((2, cx + 2 * REACH, cz, cy), jnp.float32),
                            pltpu.SemaphoreType.DMA((3,))],
            compiler_params=pltpu.CompilerParams(vmem_limit_bytes=67043328 - (10480 << 10)),
            name="prep",
        )(packed, source_fine, source_coarse)

        made = pl.pallas_call(
            functools.partial(table_kernel, tiles, fine_sizes, coarse_sizes),
            out_shape=level_shapes(nx, ny) + level_shapes(cx, cy)[:3],
            in_specs=[VMEM] * 4 + [HBM],
            out_specs=(VMEM,) * 7,
            scratch_shapes=[pltpu.VMEM((2, TERMS, LANES), jnp.float32),
                            pltpu.VMEM((TERMS, full_y), jnp.float32)],
            compiler_params=limit(8),
            name="tables",
        )(mode_x, mode_y, mode_z, source_fine, par)

        side_a = lax.ppermute(side_a, axes, beside(bits[0], True))
        side_b = lax.ppermute(side_b, axes, beside(bits[1], False))
        more = []
        for d in others:
            more.append(lax.ppermute(par, "member", [(i, i ^ (2 * d)) for i in range(members)]))
        par, made = lax.optimization_barrier((par, made))
        of_fine, of_coarse = made[:4], made[4:]
        par = jnp.concatenate([par, side_a[rows:, :LANES], side_b[rows:]] + more, axis=0)
        twin = lax.ppermute(par, "member", [(i, i ^ 1) for i in range(members)])

        groups = tiles * n_coarse * cz // LANES
        early = max(groups // 2, 1)
        part = jax.ShapeDtypeStruct((cx, cz, cy), jnp.float32)
        near, force = pl.pallas_call(
            functools.partial(coarse_near_kernel, tiles, range(early), coarse_sizes, n_fine,
                              n_coarse, (height, EDGE * 2, rows // cz)),
            out_shape=(part, level_shapes(cx, cy)[3]),
            in_specs=[VMEM] * 7,
            out_specs=(VMEM, VMEM),
            scratch_shapes=scratch(early, cx, cy, cx),
            compiler_params=limit(16),
            name="coarse_near",
        )(*of_coarse, source_coarse, par, side_a, side_b)

        fine_groups = tiles * n_fine * nz // LANES
        fine = pl.pallas_call(
            functools.partial(fine_kernel, tiles, fine_groups, fine_sizes, strip, n_fine),
            out_shape=jax.ShapeDtypeStruct((nx // 2, nz // 2, ny // 2), jnp.float32),
            in_specs=[VMEM] * 7 + [HBM],
            out_specs=VMEM,
            scratch_shapes=scratch(2 * fine_groups, nx, ny, nx // 2)
            + [pltpu.VMEM((REACH, height, LANES), jnp.float32)],
            compiler_params=limit(24),
            name="fine_smooth",
        )(*of_fine, par, twin, side_a, near)
        arrived = lax.ppermute(fine, axes, everywhere(owner))

        far = pl.pallas_call(
            functools.partial(coarse_far_kernel, tiles, range(early, groups), range(groups),
                              coarse_sizes, n_fine, n_coarse),
            out_shape=part,
            in_specs=[VMEM] * 7,
            out_specs=VMEM,
            scratch_shapes=scratch(2 * groups - early, cx, cy, cx),
            compiler_params=limit(16),
            name="coarse_far",
        )(*of_coarse, force, par, twin, near)
        return arrived + far

    return jax.shard_map(
        body,
        mesh=mesh,
        in_specs=(
            P("member", None), P("member", None), P("member"), P("member"),
            P(), P(), P(), P("tile", None, None), P(None, None, "tile"),
        ),
        out_specs=P("member", None, "tile"),
        check_vma=False,
    )
```
